128 devices in a mesh: rows: 16 (over z, x), heads: 8 (over y, core).
Axes of the slice: x: 4, y: 4, z: 4, core: 2. Of those that a mesh axis runs over, the one named last changes fastest.
Arguments:
- stream: bfloat16 [256, 4096], P('rows', 'heads'), may hold values from -6 to 6
- self_query: bfloat16 [256, 8192], P('rows', 'heads'), may hold values from -200 to 200
- new_kv: bfloat16 [256, 8, 256], P('rows', 'heads'), may hold values from -8 to 8
- cache_pool: bfloat16 [1536, 64, 8, 256], P('rows', None, 'heads'), may hold values from -8 to 8
- page_table: int32 [256, 6], P('rows'), may hold values from 0 to 95, as said below
- lengths: int32 [256], P('rows'), may hold values from 1 to 383, as said below
- migration: int32 [256, 2], P('rows'), may hold values from -1 to 15, as said below
- image_of: int32 [256], replicated, may hold values from 0 to 15, as said below
- cross_query: bfloat16 [256, 8192], P('rows', 'heads'), may hold values from -200 to 200
- image_cache: bfloat16 [16, 2048, 8, 256], P(None, 'rows', 'heads'), may hold values from -8 to 8
- self_output: bfloat16 [8192, 4096], P('heads'), may hold values from -0.125 to 0.125
- cross_output: bfloat16 [8192, 4096], P('heads'), may hold values from -0.5 to 0.5
- cross_gate: float32 [1], replicated, may hold values from 0.3 to 1.2
Outputs:
- self_update: bfloat16 [256, 4096], P('rows', 'heads')
- cross_update: bfloat16 [256, 4096], P('rows', 'heads')
- new_cache: bfloat16 [256, 384, 8, 256], P('rows', None, 'heads')
The draws below stay inside these ranges and needn't reach their ends.
Inputs may be any that keep to these rules, and one draw needn't show every extreme that they name: `page_table`: each index of rows lists, over its 16 rows, every page number of its block of 96 pages exactly once. The new token of row r goes to position lengths[r]. `migration`: A finished row gives (-1, -1), a live row (destination index along rows, slot). No slot of a destination is named twice. The slots of a destination form aligned groups of 2, each group named only by rows of one index of rows; the rows of one index go to 8 different destinations, at most 2 rows to each, and some index sends 2 live rows to one destination. Some destination has all 16 slots named. `image_of`: every image is the image of exactly 16 rows.
All inputs are finite; a program needn't handle non-finite values.
Results may differ from the reference program's by a relative error of at most 0.0085.
Values may be sent and summed in bfloat16 or wider, within the bound.
No kernel may reach another device: no remote copies, remote signals or barrier semaphores. Data moves between devices by JAX's collectives and lax.ppermute only.
A program may use at most 128 MiB of HBM per device.

```python
import math
import jax
import jax.numpy as jnp
from jax import lax

QH = 64
KVH = 8
HD = 128
DW = 4096
ROWS_DEV = 16
PG = 64
MAXPG = 6
GROUP = 16
ROWS = 256
HIST = 384
IMAGES = 16
IMG_TOK = 2048


def distinct_order(subkey, count_rows, count):
    scores = jax.random.randint(subkey, (count_rows, count), 0, 1 << 20) * count + jnp.arange(count, dtype=jnp.int32)[None, :]
    return jnp.argsort(scores, axis=1).astype(jnp.int32)


def offset_order(subkey, devices):
    steps = jnp.arange(devices, dtype=jnp.int32)
    scores = jax.random.randint(subkey, (devices,), 0, 1 << 20) * devices + steps
    scores = jnp.where(steps == devices // 2, -2, scores)
    scores = jnp.where(steps == devices - 1, -1, scores)
    return jnp.argsort(scores).astype(jnp.int32)


def layout(key):
    devices = ROWS // ROWS_DEV
    per_pair = max(2, 2 * ROWS_DEV // devices)
    groups = ROWS_DEV // per_pair
    pool_pages = ROWS_DEV * MAXPG
    page_table = distinct_order(jax.random.fold_in(key, 101), devices, pool_pages).reshape(ROWS, MAXPG)
    image_of = (distinct_order(jax.random.fold_in(key, 102), 1, ROWS)[0] // GROUP).astype(jnp.int32)
    offsets = offset_order(jax.random.fold_in(key, 103), devices)[:groups]
    order_rows = distinct_order(jax.random.fold_in(key, 104), devices, ROWS_DEV)
    inverse = jnp.argsort(order_rows, axis=1).astype(jnp.int32)
    source = jnp.arange(devices, dtype=jnp.int32)[:, None]
    target_dev = ((source - offsets[inverse // per_pair]) % devices).astype(jnp.int32)
    filled = jax.random.randint(jax.random.fold_in(key, 105), (devices,), 0, 4) == 0
    forced = jax.random.randint(jax.random.fold_in(key, 106), (), 0, devices)
    filled = filled | (jnp.arange(devices, dtype=jnp.int32) == forced)
    living = filled[target_dev] | (jax.random.randint(jax.random.fold_in(key, 107), (devices, ROWS_DEV), 0, 100) < 80)
    migration = jnp.stack([jnp.where(living, target_dev, -1), jnp.where(living, inverse, -1)], axis=-1).reshape(ROWS, 2).astype(jnp.int32)
    lengths = jax.random.randint(jax.random.fold_in(key, 108), (ROWS,), 1, HIST).astype(jnp.int32)
    return (page_table, image_of, migration, lengths)


def bounded_normal(subkey, shape_of, spread_factor):
    return jnp.clip(jax.random.normal(subkey, shape_of, jnp.float32), -6.0, 6.0) * spread_factor


def floats(key):
    self_query = bounded_normal(jax.random.fold_in(key, 201), (ROWS, QH, HD), 2.0)
    new_kv = bounded_normal(jax.random.fold_in(key, 202), (ROWS, KVH, 2 * HD), 1.0)
    cache_pool = bounded_normal(jax.random.fold_in(key, 203), (ROWS * MAXPG, PG, KVH, 2 * HD), 1.0)
    cross_query = bounded_normal(jax.random.fold_in(key, 204), (ROWS, QH, HD), 2.0)
    image_cache = bounded_normal(jax.random.fold_in(key, 205), (IMAGES, IMG_TOK, KVH, 2 * HD), 1.0)
    return (self_query.reshape(ROWS, QH * HD), new_kv, cache_pool, cross_query.reshape(ROWS, QH * HD), image_cache)


def draw_self_query(key, part):
    return floats(key)[0].astype(jnp.bfloat16)


def draw_new_kv(key, part):
    return floats(key)[1].astype(jnp.bfloat16)


def draw_cache_pool(key, part):
    return floats(key)[2].astype(jnp.bfloat16)


def draw_cross_query(key, part):
    return floats(key)[3].astype(jnp.bfloat16)


def draw_image_cache(key, part):
    return floats(key)[4].astype(jnp.bfloat16)


def draw_page_table(key, part):
    return layout(key)[0]


def draw_image_of(key, part):
    return layout(key)[1]


def draw_migration(key, part):
    return layout(key)[2]


def draw_lengths(key, part):
    return layout(key)[3]


def block_scale(stream_key, shape, pieces, low, top_value):
    gain = 1.0
    for axis_at, shards_of in pieces:
        draws = jax.random.uniform(jax.random.fold_in(jax.random.fold_in(stream_key, 6), axis_at), (shards_of,), jnp.float32, low / len(pieces), top_value / len(pieces))
        gain = gain * jnp.repeat(jnp.exp(draws), shape[axis_at] // shards_of).reshape((-1,) + (1,) * (len(shape) - 1 - axis_at))
    return gain


def centred(stream_key, dims, spread, limit, pieces=(), kind=jnp.bfloat16):
    entries = spread * jax.random.normal(stream_key, dims, jnp.float32)
    if pieces:
        entries = entries * block_scale(stream_key, dims, pieces, -0.22, 0.18)
    return jnp.clip(entries, -limit, limit).astype(kind)


def setup_inputs(seed: int = 0) -> dict:
    key_list = jax.random.split(jax.random.key(seed), 14)
    return {
        "stream": centred(key_list[0], (ROWS, DW), 1.0, 6.0, ((0, 16), (1, 8))),
        "self_query": draw_self_query(jax.random.fold_in(key_list[13], 71), 0),
        "new_kv": draw_new_kv(jax.random.fold_in(key_list[13], 71), 0),
        "cache_pool": draw_cache_pool(jax.random.fold_in(key_list[13], 71), 0),
        "page_table": draw_page_table(jax.random.fold_in(key_list[13], 71), 0),
        "lengths": draw_lengths(jax.random.fold_in(key_list[13], 71), 0),
        "migration": draw_migration(jax.random.fold_in(key_list[13], 71), 0),
        "image_of": draw_image_of(jax.random.fold_in(key_list[13], 71), 0),
        "cross_query": draw_cross_query(jax.random.fold_in(key_list[13], 71), 0),
        "image_cache": draw_image_cache(jax.random.fold_in(key_list[13], 71), 0),
        "self_output": centred(key_list[10], (QH * HD, DW), (QH * HD // 4) ** -0.5, 0.125, ((0, 8),)),
        "cross_output": centred(key_list[11], (QH * HD, DW), (QH * HD // 64) ** -0.5, 0.5, ((0, 8),)),
        "cross_gate": jnp.clip(jax.random.uniform(key_list[12], (1,), jnp.float32, 0.3, 1.2), 0.3, 1.2),
    }


def attend_row(queries, keys, values, visible):
    scores = jnp.einsum('kgd,tkd->kgt', queries, keys) * (1.0 / math.sqrt(HD))
    scores = jnp.where(visible[None, None, :], scores, -1e+30)
    highest = lax.optimization_barrier(jnp.max(scores, axis=-1, keepdims=True))
    weights = jnp.exp(scores - highest)
    weight_sum = lax.optimization_barrier(jnp.sum(weights, axis=-1))
    blended = jnp.einsum('kgt,tkd->kgd', weights, values)
    return (blended / weight_sum[..., None]).reshape(-1).astype(jnp.bfloat16)

def reference(stream, self_query, new_kv, cache_pool, page_table, lengths, migration, image_of, cross_query, image_cache, self_output, cross_output, cross_gate):
    group_size = QH // KVH
    device = jnp.arange(ROWS, dtype=jnp.int32) // ROWS_DEV
    page_index = (page_table + (device * (ROWS_DEV * MAXPG))[:, None]).astype(jnp.int32)
    taken = cache_pool[page_index.reshape(-1)].reshape(ROWS, HIST, KVH, 2 * HD)
    position = jnp.arange(HIST, dtype=jnp.int32)[None, :]
    written = jnp.where((position == lengths[:, None])[:, :, None, None], new_kv[:, None], taken)
    visible = position <= lengths[:, None]

    def self_one(element):
        query_row, rows_kv, visible_row = element
        grouped = query_row.astype(jnp.float32).reshape(KVH, group_size, HD)
        return attend_row(grouped, rows_kv[..., :HD].astype(jnp.float32), rows_kv[..., HD:].astype(jnp.float32), visible_row)
    self_attended = lax.map(self_one, (self_query, written, visible))
    everything = jnp.ones((IMG_TOK,), dtype=bool)

    def cross_one(element):
        query_row, image_id = element
        tokens = lax.dynamic_index_in_dim(image_cache, image_id, 0, keepdims=False)
        grouped = query_row.astype(jnp.float32).reshape(KVH, group_size, HD)
        return attend_row(grouped, tokens[..., :HD].astype(jnp.float32), tokens[..., HD:].astype(jnp.float32), everything)
    cross_attended = lax.map(cross_one, (cross_query, image_of))
    self_sum = jnp.dot(self_attended, self_output, preferred_element_type=jnp.float32)
    cross_sum = jnp.dot(cross_attended, cross_output, preferred_element_type=jnp.float32)
    self_rows = (stream.astype(jnp.float32) + self_sum).astype(jnp.bfloat16)
    cross_rows = (jnp.tanh(cross_gate[0]) * cross_sum).astype(jnp.bfloat16)
    target = jnp.where(migration[:, 0] >= 0, migration[:, 0] * ROWS_DEV + migration[:, 1], ROWS).astype(jnp.int32)
    self_update = jnp.zeros((ROWS, DW), jnp.bfloat16).at[target].set(self_rows, mode='drop')
    cross_update = jnp.zeros((ROWS, DW), jnp.bfloat16).at[target].set(cross_rows, mode='drop')
    new_cache = jnp.zeros((ROWS, HIST, KVH, 2 * HD), jnp.bfloat16).at[target].set(written, mode='drop')
    return (self_update, cross_update, new_cache)
```

```python
import functools
import math

import jax
import jax.numpy as jnp
from jax import lax
from jax.experimental import pallas as pl
from jax.experimental.pallas import tpu as pltpu
from jax.sharding import PartitionSpec as P

very_low = -1e30
bf16 = jnp.bfloat16
f32 = jnp.float32
i32 = jnp.int32
LANES = 128
VMEM = pltpu.VMEM
SMEM = pltpu.SMEM


def vmem():
    return pl.BlockSpec(memory_space=VMEM)


def smem():
    return pl.BlockSpec(memory_space=SMEM)


def anywhere():
    return pl.BlockSpec(memory_space=pl.ANY)


def iota(shape, dim):
    return lax.broadcasted_iota(i32, shape, dim)


def onto(a, b):
    return lax.dot_general(a, b, (((0,), (0,)), ((), ())), preferred_element_type=f32)


def against(a, b):
    return lax.dot_general(a, b, (((1,), (1,)), ((), ())), preferred_element_type=f32)


def ranks_of(mig_ref, count):
    targets = [mig_ref[0, r] for r in range(count)]
    ranks = []
    for r in range(count):
        rank = jnp.int32(0)
        for e in range(r):
            rank = rank + (targets[e] == targets[r]).astype(i32)
        ranks.append(jnp.minimum(rank, 1))
    return targets, ranks


def pack_body(rows, mig_ref, query_ref, out_ref):
    targets, ranks = ranks_of(mig_ref, rows)
    width = query_ref.shape[1]
    sub, lane = iota((rows, LANES), 0), iota((rows, LANES), 1)
    about = jnp.full((rows, LANES), -1, i32)
    for r in range(rows):
        slot = jnp.where(targets[r] >= 0, targets[r] * rows + mig_ref[1, r], -1)
        about = jnp.where((sub == r) & (lane == 0), slot, about)
        about = jnp.where((sub == r) & (lane == 1), ranks[r], about)
    about = about.astype(f32).astype(bf16)
    for d in range(out_ref.shape[0]):
        out_ref[d, :, 0:width] = query_ref[...]
        out_ref[d, :, width : width + LANES] = about


def own_body(
    rows, pages, page_len, scale, pt_ref, len_ref, mig_ref, pool, kv_ref, query_ref, buf, att_ref,
    held, in_sem, out_sem,
):
    targets, ranks = ranks_of(mig_ref, rows)
    history = pages * page_len
    head = kv_ref.shape[1] // 2
    heads = query_ref.shape[1]
    for r in range(rows):
        for p in range(pages):
            pltpu.make_async_copy(
                pool.at[pt_ref[p, r]], held.at[r, pl.ds(p * page_len, page_len)], in_sem.at[r, p]
            ).start()

    def sending(r):
        place = jnp.maximum(targets[r], 0) * 2 + ranks[r]
        return pltpu.make_async_copy(held.at[r], buf.at[place], out_sem.at[r])

    for r in range(rows):
        for p in range(pages):
            pltpu.make_async_copy(
                pool.at[pt_ref[p, r]], held.at[r, pl.ds(p * page_len, page_len)], in_sem.at[r, p]
            ).wait()
        length = len_ref[r]
        base = pl.multiple_of((length // 16) * 16, 16)
        block = held[r, pl.ds(base, 16), :].astype(f32)
        token = kv_ref[r : r + 1, :].astype(f32)
        here = iota(block.shape, 0) == length - base
        held[r, pl.ds(base, 16), :] = jnp.where(here, token, block).astype(bf16)

        @pl.when(targets[r] >= 0)
        def _():
            sending(r).start()

    for r in range(rows):
        scores = against(query_ref[r], held[r, :, 0:head]) * scale
        scores = jnp.where(iota((heads, history), 1) <= len_ref[r], scores, very_low)
        weights = jnp.exp(scores - jnp.max(scores, axis=1, keepdims=True))
        total = jnp.sum(weights, axis=1, keepdims=True)
        blended = jnp.dot(weights.astype(bf16), held[r, :, head:], preferred_element_type=f32)
        att_ref[r * heads : (r + 1) * heads, :] = (blended / total).astype(bf16)

    for r in range(rows):

        @pl.when(targets[r] >= 0)
        def _():
            sending(r).wait()


def cross_body(
    rows, scale, mig_ref, asked_ref, image_col_ref, image_row_ref, cache_ref, att_ref, stream_ref,
    out_ref, sorted_ref, part_ref,
):
    images, tokens, both = cache_ref.shape
    head = both // 2
    everyone = asked_ref.shape[0]
    width = asked_ref.shape[1] - LANES
    heads = width // head
    group = everyone // images
    square = (everyone, everyone)
    image_col = image_col_ref[...]
    same = (image_col == image_row_ref[...]) & (iota(square, 1) < iota(square, 0))
    rank = jnp.sum(jnp.where(same, 1.0, 0.0), axis=1, keepdims=True).astype(i32)
    by_image = (iota(square, 1) == image_col * group + rank).astype(f32).astype(bf16)
    slot = asked_ref[:, width : width + 1].astype(f32).astype(i32)
    by_slot = (iota(square, 1) == slot).astype(f32).astype(bf16)
    sorted_ref[...] = onto(by_image, asked_ref[:, 0:width]).astype(bf16)
    order = onto(by_slot, by_image).astype(bf16)
    stacked = heads * group
    lane = iota((stacked, LANES), 1)
    head_of = iota((stacked, LANES), 0) // group
    for i in range(images):
        at = slice(i * group, (i + 1) * group)
        queries = jnp.concatenate(
            [sorted_ref[at, h * head : (h + 1) * head] for h in range(heads)], axis=0
        )
        scores = against(queries, cache_ref[i, :, 0:head]) * scale
        top = jnp.max(scores, axis=1, keepdims=True)
        top_hi = top.astype(bf16).astype(f32)
        top_lo = (top - top_hi).astype(bf16).astype(f32)
        weights = jnp.exp(scores - (top_hi + top_lo))
        total = jnp.sum(weights, axis=1, keepdims=True)
        total_hi = total.astype(bf16).astype(f32)
        total_lo = (total - total_hi).astype(bf16).astype(f32)
        blended = jnp.dot(weights.astype(bf16), cache_ref[i, :, head:], preferred_element_type=f32)
        blended = (blended / total).astype(bf16)
        about = jnp.zeros((stacked, LANES), f32)
        for n, stat in enumerate((top_hi, top_lo, total_hi, total_lo)):
            about = jnp.where(lane == n * heads + head_of, stat, about)
        packed = about[0:group]
        for h in range(1, heads):
            packed = packed + about[h * group : (h + 1) * group]
        for h in range(heads):
            part_ref[at, h * head : (h + 1) * head] = blended[h * group : (h + 1) * group]
        part_ref[at, width : width + LANES] = packed.astype(bf16)
    out_ref[:, 0 : width + LANES] = jnp.dot(
        order, part_ref[...], preferred_element_type=f32
    ).astype(bf16)
    targets, ranks = ranks_of(mig_ref, rows)
    chunks = stream_ref.shape[0] // rows
    lane_a = iota((1, rows * heads), 1)
    lane_s = iota((1, rows * chunks), 1)
    to_a = jnp.full(lane_a.shape, -1, i32)
    to_s = jnp.full(lane_s.shape, -1, i32)
    for r in range(rows):
        live = targets[r] >= 0
        base_a = jnp.where(live, targets[r] * rows + ranks[r] * heads, -rows * 64)
        base_s = jnp.where(live, targets[r] * rows + ranks[r] * chunks, -rows * 64)
        to_a = jnp.where(lane_a // heads == r, base_a + lane_a % heads, to_a)
        to_s = jnp.where(lane_s // chunks == r, base_s + lane_s % chunks, to_s)
    pick_a = (iota((everyone, rows * heads), 0) == to_a).astype(f32).astype(bf16)
    pick_s = (iota((everyone, rows * chunks), 0) == to_s).astype(f32).astype(bf16)
    at = width + LANES
    out_ref[:, at : at + LANES] = jnp.dot(
        pick_a, att_ref[...], preferred_element_type=f32
    ).astype(bf16)
    out_ref[:, at + LANES : at + 2 * LANES] = jnp.dot(
        pick_s, stream_ref[...], preferred_element_type=f32
    ).astype(bf16)


def settle_body(
    rows, me_ref, asked_ref, came_ref, att_ref, cross_ref, stream_ref, source_ref, coef_ref
):
    sources = came_ref.shape[0]
    everyone = asked_ref.shape[0]
    width = asked_ref.shape[1] - LANES
    heads = width // LANES
    chunks = stream_ref.shape[1] // LANES
    tall = (everyone, LANES)
    slot = asked_ref[:, width : width + 1].astype(f32).astype(i32)
    rank = asked_ref[:, width + 1 : width + 2].astype(f32).astype(i32)
    lane = iota(tall, 1)
    source = iota(tall, 0) // rows
    match = ((slot - me_ref[0] * rows == lane) & (lane < rows)).astype(f32).astype(bf16)
    facts = jnp.where(lane == 0, source * 2 + rank, 0)
    facts = jnp.where(lane == 1, source * rows + rank * heads, facts)
    facts = jnp.where(lane == 2, source * rows + rank * chunks, facts)
    facts = jnp.where(lane == 3, 1, facts).astype(f32).astype(bf16)
    by_lane = onto(facts, match)
    source_ref[...] = jnp.where(by_lane[3:4] > 0.5, by_lane[0:1], -1.0).astype(i32) + jnp.zeros(
        source_ref.shape, i32
    )
    by_row = onto(match, facts)[0:rows]
    live = by_row[:, 3:4] > 0.5
    base_a = jnp.where(live, by_row[:, 1:2], -4096.0).astype(i32)
    base_s = jnp.where(live, by_row[:, 2:3], -4096.0).astype(i32)
    column = iota((rows, everyone), 1)
    at = width + LANES
    own_a = came_ref[:, :, at : at + LANES].reshape(everyone, LANES)
    own_s = came_ref[:, :, at + LANES : at + 2 * LANES].reshape(everyone, LANES)
    for h in range(heads):
        pick = (column == base_a + h).astype(f32).astype(bf16)
        att_ref[:, h * LANES : (h + 1) * LANES] = jnp.dot(
            pick, own_a, preferred_element_type=f32
        ).astype(bf16)
    for c in range(chunks):
        pick = (column == base_s + c).astype(f32).astype(bf16)
        stream_ref[:, c * LANES : (c + 1) * LANES] = jnp.dot(
            pick, own_s, preferred_element_type=f32
        ).astype(bf16)
    highest = None
    for s in range(sources):
        about = came_ref[s, :, width : width + LANES].astype(f32)
        about = about + pltpu.roll(about, LANES - heads, 1)
        coef_ref[s] = about
        highest = about if s == 0 else jnp.maximum(highest, about)
    total = jnp.zeros((rows, LANES), f32)
    for s in range(sources):
        about = coef_ref[s]
        share = jnp.exp(about - highest) * pltpu.roll(about, LANES - 2 * heads, 1)
        coef_ref[s] = share
        total = total + share
    over = jnp.where(live, 1.0 / total, 0.0)
    for h in range(heads):
        blended = jnp.zeros((rows, LANES), f32)
        for s in range(sources):
            part = came_ref[s, :, h * LANES : (h + 1) * LANES].astype(f32)
            blended = blended + coef_ref[s][:, h : h + 1] * part
        blended = jnp.where(live, blended * over[:, h : h + 1], 0.0)
        cross_ref[:, h * LANES : (h + 1) * LANES] = blended.astype(bf16)


def project_body(me_ref, att_ref, cross_ref, self_w_ref, cross_w_ref, out_ref):
    rows = att_ref.shape[0]
    out_ref[0, 0:rows] = jnp.dot(att_ref[...], self_w_ref[...], preferred_element_type=f32)
    out_ref[0, rows : 2 * rows] = jnp.dot(
        cross_ref[...], cross_w_ref[...], preferred_element_type=f32
    )


def place_body(source_ref, came_ref, out_ref):
    named = source_ref[0, pl.program_id(0)] >= 0

    @pl.when(named)
    def _():
        out_ref[...] = came_ref[...]

    @pl.when(jnp.logical_not(named))
    def _():
        out_ref[...] = jnp.zeros_like(out_ref)


def per_device(
    stream,
    self_query,
    new_kv,
    cache_pool,
    page_table,
    lengths,
    migration,
    image_of,
    cross_query,
    image_cache,
    self_output,
    cross_output,
    cross_gate,
):
    rows, width = cross_query.shape
    devices = lax.axis_size("rows")
    columns = lax.axis_size("heads")
    everyone = rows * devices
    pages = page_table.shape[1]
    pool_pages, page_len, _, both = cache_pool.shape
    head = both // 2
    heads = width // head
    history = pages * page_len
    images, tokens = image_cache.shape[:2]
    part = stream.shape[1]
    chunks = part // LANES
    scale = 1.0 / math.sqrt(head)
    out_width = self_output.shape[1]
    shape = jax.ShapeDtypeStruct
    mig = migration.T
    my_row = lax.axis_index("rows").astype(i32)[None]
    my_column = lax.axis_index("heads").astype(i32)[None]

    packed = pl.pallas_call(
        functools.partial(pack_body, rows),
        out_shape=shape((devices, rows, width + LANES), bf16),
        in_specs=[smem(), vmem()],
        out_specs=vmem(),
        name="pack",
    )(mig, cross_query)
    asked = lax.all_to_all(packed, "rows", 0, 0, tiled=True).reshape(everyone, width + LANES)

    buffer, attended = pl.pallas_call(
        functools.partial(own_body, rows, pages, page_len, scale),
        out_shape=(
            shape((devices * 2, history, both), bf16),
            shape((rows * heads, head), bf16),
        ),
        in_specs=[smem(), smem(), smem(), anywhere(), vmem(), vmem()],
        out_specs=(anywhere(), vmem()),
        scratch_shapes=[
            VMEM((rows, history, both), bf16),
            pltpu.SemaphoreType.DMA((rows, pages)),
            pltpu.SemaphoreType.DMA((rows,)),
        ],
        cost_estimate=pl.CostEstimate(
            flops=4 * rows * heads * history * head,
            bytes_accessed=4 * rows * history * both,
            transcendentals=rows * heads * history,
        ),
        name="own",
    )(
        page_table.T,
        lengths,
        mig,
        cache_pool.reshape(pool_pages, page_len, both),
        new_kv.reshape(rows, both),
        self_query.reshape(rows, heads, head),
    )

    message_width = width + 3 * LANES
    message = pl.pallas_call(
        functools.partial(cross_body, rows, scale),
        out_shape=shape((everyone, message_width), bf16),
        in_specs=[smem(), vmem(), vmem(), vmem(), vmem(), vmem(), vmem()],
        out_specs=vmem(),
        scratch_shapes=[VMEM((everyone, width), bf16), VMEM((everyone, width + LANES), bf16)],
        cost_estimate=pl.CostEstimate(
            flops=4 * everyone * heads * tokens * head + 8 * everyone * everyone * width,
            bytes_accessed=2 * images * tokens * both + 4 * everyone * width,
            transcendentals=everyone * heads * tokens,
        ),
        name="cross",
    )(
        mig,
        asked,
        image_of.reshape(everyone, 1),
        image_of.reshape(1, everyone),
        image_cache.reshape(images, tokens, both),
        attended,
        stream.reshape(rows * chunks, LANES),
    )
    came = lax.all_to_all(
        message.reshape(devices, rows, message_width), "rows", 0, 0, tiled=True
    )
    buffer, came = lax.optimization_barrier((buffer, came))
    moved = lax.all_to_all(
        buffer.reshape(devices, 2 * history, both), "rows", 0, 0, tiled=True
    )

    slot_attended, slot_cross, slot_stream, source = pl.pallas_call(
        functools.partial(settle_body, rows),
        out_shape=(
            shape((rows, width), bf16),
            shape((rows, width), bf16),
            shape((rows, part), bf16),
            shape((8, LANES), i32),
        ),
        in_specs=[smem(), vmem(), vmem()],
        out_specs=(vmem(), vmem(), vmem(), vmem()),
        scratch_shapes=[VMEM((devices, rows, LANES), f32)],
        cost_estimate=pl.CostEstimate(
            flops=4 * everyone * width,
            bytes_accessed=4 * everyone * width,
            transcendentals=everyone * LANES,
        ),
        name="combine",
    )(my_row, asked, came)

    parts = pl.pallas_call(
        project_body,
        grid_spec=pltpu.PrefetchScalarGridSpec(
            num_scalar_prefetch=1,
            grid=(columns,),
            in_specs=[
                pl.BlockSpec((rows, width), lambda o, me: (0, 0)),
                pl.BlockSpec((rows, width), lambda o, me: (0, 0)),
                pl.BlockSpec((width, part), lambda o, me: (0, lax.rem(me[0] + o, columns))),
                pl.BlockSpec((width, part), lambda o, me: (0, lax.rem(me[0] + o, columns))),
            ],
            out_specs=pl.BlockSpec((1, 2 * rows, part), lambda o, me: (o, 0, 0)),
        ),
        out_shape=shape((columns, 2 * rows, part), f32),
        cost_estimate=pl.CostEstimate(
            flops=4 * rows * width * out_width,
            bytes_accessed=4 * width * out_width,
            transcendentals=0,
        ),
        name="project",
    )(my_column, slot_attended, slot_cross, self_output, cross_output)
    summed = parts[0]
    for o in range(1, columns):
        summed = summed + lax.ppermute(
            parts[o], "heads", [(c, (c + o) % columns) for c in range(columns)]
        )
    self_update = (slot_stream.astype(f32) + summed[:rows]).astype(bf16)
    cross_update = (jnp.tanh(cross_gate[0]) * summed[rows:]).astype(bf16)

    new_cache = pl.pallas_call(
        place_body,
        grid_spec=pltpu.PrefetchScalarGridSpec(
            num_scalar_prefetch=1,
            grid=(rows,),
            in_specs=[
                pl.BlockSpec(
                    (1, history, both), lambda t, source: (jnp.maximum(source[0, t], 0), 0, 0)
                )
            ],
            out_specs=pl.BlockSpec((1, history, both), lambda t, source: (t, 0, 0)),
        ),
        out_shape=shape((rows, history, both), bf16),
        cost_estimate=pl.CostEstimate(
            flops=0, bytes_accessed=4 * rows * history * both, transcendentals=0
        ),
        name="place",
    )(source, moved.reshape(devices * 2, history, both))
    return (self_update, cross_update, new_cache.reshape(rows, history, 1, both))


def solution(mesh):
    in_specs = (
        P("rows", "heads"),
        P("rows", "heads"),
        P("rows", "heads", None),
        P("rows", None, "heads", None),
        P("rows", None),
        P("rows"),
        P("rows", None),
        P(),
        P("rows", "heads"),
        P(None, "rows", "heads", None),
        P("heads", None),
        P("heads", None),
        P(),
    )
    out_specs = (P("rows", "heads"), P("rows", "heads"), P("rows", None, "heads", None))
    return jax.shard_map(
        per_device, mesh=mesh, in_specs=in_specs, out_specs=out_specs, check_vma=False
    )
```

```python
import functools
import math

import jax
import jax.numpy as jnp
from jax import lax
from jax.experimental import pallas as pl
from jax.experimental.pallas import tpu as pltpu
from jax.sharding import PartitionSpec as P

very_low = -1e30
bf16 = jnp.bfloat16
f32 = jnp.float32
i32 = jnp.int32
LANES = 128
VMEM = pltpu.VMEM
SMEM = pltpu.SMEM


def vmem():
    return pl.BlockSpec(memory_space=VMEM)


def smem():
    return pl.BlockSpec(memory_space=SMEM)


def anywhere():
    return pl.BlockSpec(memory_space=pl.ANY)


def iota(shape, dim):
    return lax.broadcasted_iota(i32, shape, dim)


def onto(a, b):
    return lax.dot_general(a, b, (((0,), (0,)), ((), ())), preferred_element_type=f32)


def against(a, b):
    return lax.dot_general(a, b, (((1,), (1,)), ((), ())), preferred_element_type=f32)


def ranks_of(mig_ref, count):
    targets = [mig_ref[0, r] for r in range(count)]
    ranks = []
    for r in range(count):
        rank = jnp.int32(0)
        for e in range(r):
            rank = rank + (targets[e] == targets[r]).astype(i32)
        ranks.append(jnp.minimum(rank, 1))
    return targets, ranks


def pack_body(rows, mig_ref, query_ref, out_ref):
    targets, ranks = ranks_of(mig_ref, rows)
    width = query_ref.shape[1]
    sub, lane = iota((rows, LANES), 0), iota((rows, LANES), 1)
    about = jnp.full((rows, LANES), -1, i32)
    for r in range(rows):
        slot = jnp.where(targets[r] >= 0, targets[r] * rows + mig_ref[1, r], -1)
        about = jnp.where((sub == r) & (lane == 0), slot, about)
        about = jnp.where((sub == r) & (lane == 1), ranks[r], about)
    about = about.astype(f32).astype(bf16)
    for d in range(out_ref.shape[0]):
        out_ref[d, :, 0:width] = query_ref[...]
        out_ref[d, :, width : width + LANES] = about


def own_body(
    rows, pages, page_len, scale, pt_ref, len_ref, mig_ref, pool, kv_ref, query_ref, early, late,
    att_ref, held, split_ref, in_sem, early_sem, late_sem,
):
    targets, ranks = ranks_of(mig_ref, rows)
    history = pages * page_len
    head = kv_ref.shape[1] // 2
    heads = query_ref.shape[1] // head
    first = early.shape[1]

    def fetching(r, p):
        return pltpu.make_async_copy(
            pool.at[pt_ref[p, r]], held.at[r, pl.ds(p * page_len, page_len)], in_sem.at[r, p]
        )

    def sending(r):
        place = jnp.maximum(targets[r], 0) * 2 + ranks[r]
        return (
            pltpu.make_async_copy(
                held.at[r, pl.ds(0, first)], early.at[place], early_sem.at[r]
            ),
            pltpu.make_async_copy(
                held.at[r, pl.ds(first, history - first)], late.at[place], late_sem.at[r]
            ),
        )

    for r in range(rows):
        for p in range(pages):
            fetching(r, p).start()
    for h in range(heads):
        split_ref[pl.ds(h, rows, stride=heads), :] = query_ref[:, h * head : (h + 1) * head].astype(
            f32
        )
    for r in range(rows):
        for p in range(pages):
            fetching(r, p).wait()
        length = len_ref[r]
        base = pl.multiple_of((length // 16) * 16, 16)
        block = held[r, pl.ds(base, 16), :].astype(f32)
        token = kv_ref[r : r + 1, :].astype(f32)
        here = iota(block.shape, 0) == length - base
        held[r, pl.ds(base, 16), :] = jnp.where(here, token, block).astype(bf16)

        @pl.when(targets[r] >= 0)
        def _():
            for copy in sending(r):
                copy.start()

    for r in range(rows):
        queries = split_ref[r * heads : (r + 1) * heads, :].astype(bf16)
        scores = against(queries, held[r, :, 0:head]) * scale
        scores = jnp.where(iota((heads, history), 1) <= len_ref[r], scores, very_low)
        weights = jnp.exp(scores - jnp.max(scores, axis=1, keepdims=True))
        total = jnp.sum(weights, axis=1, keepdims=True)
        blended = jnp.dot(weights.astype(bf16), held[r, :, head:], preferred_element_type=f32)
        att_ref[r * heads : (r + 1) * heads, :] = (blended / total).astype(bf16)

    for r in range(rows):

        @pl.when(targets[r] >= 0)
        def _():
            for copy in sending(r):
                copy.wait()


def cross_body(
    rows, scale, mig_ref, asked_ref, image_row_ref, cache_ref, att_ref, stream_ref, out_ref,
    sorted_ref, part_ref, split_ref,
):
    images, tokens, both = cache_ref.shape
    head = both // 2
    everyone = asked_ref.shape[0]
    width = asked_ref.shape[1] - LANES
    heads = width // head
    group = everyone // images
    square = (everyone, everyone)
    image_row = image_row_ref[...]
    diagonal = iota(square, 1) == iota(square, 0)
    image_col = jnp.sum(
        jnp.where(diagonal, image_row.astype(f32), 0.0), axis=1, keepdims=True
    ).astype(i32)
    same = (image_col == image_row) & (iota(square, 1) < iota(square, 0))
    rank = jnp.sum(jnp.where(same, 1.0, 0.0), axis=1, keepdims=True).astype(i32)
    by_image = (iota(square, 1) == image_col * group + rank).astype(f32).astype(bf16)
    slot = asked_ref[:, width : width + 1].astype(f32).astype(i32)
    by_slot = (iota(square, 1) == slot).astype(f32).astype(bf16)
    sorted_ref[...] = onto(by_image, asked_ref[:, 0:width]).astype(bf16)
    order = onto(by_slot, by_image).astype(bf16)
    stacked = heads * group
    lane = iota((stacked, LANES), 1)
    head_of = iota((stacked, LANES), 0) // group
    for i in range(images):
        at = slice(i * group, (i + 1) * group)
        queries = jnp.concatenate(
            [sorted_ref[at, h * head : (h + 1) * head] for h in range(heads)], axis=0
        )
        scores = against(queries, cache_ref[i, :, 0:head]) * scale
        top = jnp.max(scores, axis=1, keepdims=True)
        top_hi = top.astype(bf16).astype(f32)
        top_lo = (top - top_hi).astype(bf16).astype(f32)
        weights = jnp.exp(scores - (top_hi + top_lo))
        total = jnp.sum(weights, axis=1, keepdims=True)
        total_hi = total.astype(bf16).astype(f32)
        total_lo = (total - total_hi).astype(bf16).astype(f32)
        blended = jnp.dot(weights.astype(bf16), cache_ref[i, :, head:], preferred_element_type=f32)
        blended = (blended / total).astype(bf16)
        about = jnp.zeros((stacked, LANES), f32)
        for n, stat in enumerate((top_hi, top_lo, total_hi, total_lo)):
            about = jnp.where(lane == n * heads + head_of, stat, about)
        packed = about[0:group]
        for h in range(1, heads):
            packed = packed + about[h * group : (h + 1) * group]
        for h in range(heads):
            part_ref[at, h * head : (h + 1) * head] = blended[h * group : (h + 1) * group]
        part_ref[at, width : width + LANES] = packed.astype(bf16)
    out_ref[:, 0 : width + LANES] = jnp.dot(
        order, part_ref[...], preferred_element_type=f32
    ).astype(bf16)
    targets, ranks = ranks_of(mig_ref, rows)
    chunks = stream_ref.shape[1] // LANES
    for c in range(chunks):
        split_ref[pl.ds(c, rows, stride=chunks), :] = stream_ref[
            :, c * LANES : (c + 1) * LANES
        ].astype(f32)
    lane_a = iota((1, rows * heads), 1)
    lane_s = iota((1, rows * chunks), 1)
    to_a = jnp.full(lane_a.shape, -1, i32)
    to_s = jnp.full(lane_s.shape, -1, i32)
    for r in range(rows):
        live = targets[r] >= 0
        base_a = jnp.where(live, targets[r] * rows + ranks[r] * heads, -rows * 64)
        base_s = jnp.where(live, targets[r] * rows + ranks[r] * chunks, -rows * 64)
        to_a = jnp.where(lane_a // heads == r, base_a + lane_a % heads, to_a)
        to_s = jnp.where(lane_s // chunks == r, base_s + lane_s % chunks, to_s)
    pick_a = (iota((everyone, rows * heads), 0) == to_a).astype(f32).astype(bf16)
    pick_s = (iota((everyone, rows * chunks), 0) == to_s).astype(f32).astype(bf16)
    at = width + LANES
    out_ref[:, at : at + LANES] = jnp.dot(
        pick_a, att_ref[...], preferred_element_type=f32
    ).astype(bf16)
    out_ref[:, at + LANES : at + 2 * LANES] = jnp.dot(
        pick_s, split_ref[...].astype(bf16), preferred_element_type=f32
    ).astype(bf16)


def settle_body(
    rows, me_ref, asked_ref, came_ref, att_ref, cross_ref, stream_ref, source_ref, coef_ref
):
    sources = came_ref.shape[0]
    everyone = asked_ref.shape[0]
    width = asked_ref.shape[1] - LANES
    heads = width // LANES
    chunks = stream_ref.shape[1] // LANES
    tall = (everyone, LANES)
    slot = asked_ref[:, width : width + 1].astype(f32).astype(i32)
    rank = asked_ref[:, width + 1 : width + 2].astype(f32).astype(i32)
    lane = iota(tall, 1)
    source = iota(tall, 0) // rows
    match = ((slot - me_ref[0] * rows == lane) & (lane < rows)).astype(f32).astype(bf16)
    facts = jnp.where(lane == 0, source * 2 + rank, 0)
    facts = jnp.where(lane == 1, source * rows + rank * heads, facts)
    facts = jnp.where(lane == 2, source * rows + rank * chunks, facts)
    facts = jnp.where(lane == 3, 1, facts).astype(f32).astype(bf16)
    by_lane = onto(facts, match)
    source_ref[...] = jnp.where(by_lane[3:4] > 0.5, by_lane[0:1], -1.0).astype(i32) + jnp.zeros(
        source_ref.shape, i32
    )
    by_row = onto(match, facts)[0:rows]
    live = by_row[:, 3:4] > 0.5
    base_a = jnp.where(live, by_row[:, 1:2], -4096.0).astype(i32)
    base_s = jnp.where(live, by_row[:, 2:3], -4096.0).astype(i32)
    column = iota((rows, everyone), 1)
    at = width + LANES
    own_a = came_ref[:, :, at : at + LANES].reshape(everyone, LANES)
    own_s = came_ref[:, :, at + LANES : at + 2 * LANES].reshape(everyone, LANES)
    for h in range(heads):
        pick = (column == base_a + h).astype(f32).astype(bf16)
        att_ref[:, h * LANES : (h + 1) * LANES] = jnp.dot(
            pick, own_a, preferred_element_type=f32
        ).astype(bf16)
    for c in range(chunks):
        pick = (column == base_s + c).astype(f32).astype(bf16)
        stream_ref[:, c * LANES : (c + 1) * LANES] = jnp.dot(
            pick, own_s, preferred_element_type=f32
        ).astype(bf16)
    highest = None
    for s in range(sources):
        about = came_ref[s, :, width : width + LANES].astype(f32)
        about = about + pltpu.roll(about, LANES - heads, 1)
        coef_ref[s] = about
        highest = about if s == 0 else jnp.maximum(highest, about)
    total = jnp.zeros((rows, LANES), f32)
    for s in range(sources):
        about = coef_ref[s]
        share = jnp.exp(about - highest) * pltpu.roll(about, LANES - 2 * heads, 1)
        coef_ref[s] = share
        total = total + share
    over = jnp.where(live, 1.0 / total, 0.0)
    for h in range(heads):
        blended = jnp.zeros((rows, LANES), f32)
        for s in range(sources):
            part = came_ref[s, :, h * LANES : (h + 1) * LANES].astype(f32)
            blended = blended + coef_ref[s][:, h : h + 1] * part
        blended = jnp.where(live, blended * over[:, h : h + 1], 0.0)
        cross_ref[:, h * LANES : (h + 1) * LANES] = blended.astype(bf16)


def project_body(me_ref, att_ref, cross_ref, self_w_ref, cross_w_ref, out_ref):
    rows = att_ref.shape[0]
    out_ref[0, 0:rows] = jnp.dot(att_ref[...], self_w_ref[...], preferred_element_type=f32)
    out_ref[0, rows : 2 * rows] = jnp.dot(
        cross_ref[...], cross_w_ref[...], preferred_element_type=f32
    )


def place_body(source_ref, early, late, out, held, early_sem, late_sem, out_sem):
    rows, history, _ = held.shape
    first = early.shape[1]

    def coming(t):
        source = jnp.maximum(source_ref[0, t], 0)
        return (
            pltpu.make_async_copy(
                early.at[source], held.at[t, pl.ds(0, first)], early_sem.at[t]
            ),
            pltpu.make_async_copy(
                late.at[source], held.at[t, pl.ds(first, history - first)], late_sem.at[t]
            ),
        )

    def leaving(t):
        return pltpu.make_async_copy(held.at[t], out.at[t], out_sem.at[t])

    for t in range(rows):

        @pl.when(source_ref[0, t] >= 0)
        def _():
            for copy in coming(t):
                copy.start()

        @pl.when(source_ref[0, t] < 0)
        def _():
            held[t] = jnp.zeros(held.shape[1:], bf16)

    for t in range(rows):

        @pl.when(source_ref[0, t] >= 0)
        def _():
            for copy in coming(t):
                copy.wait()

        leaving(t).start()
    for t in range(rows):
        leaving(t).wait()


def per_device(
    stream,
    self_query,
    new_kv,
    cache_pool,
    page_table,
    lengths,
    migration,
    image_of,
    cross_query,
    image_cache,
    self_output,
    cross_output,
    cross_gate,
):
    rows, width = cross_query.shape
    devices = lax.axis_size("rows")
    columns = lax.axis_size("heads")
    everyone = rows * devices
    pages = page_table.shape[1]
    pool_pages, page_len, _, both = cache_pool.shape
    head = both // 2
    heads = width // head
    history = pages * page_len
    images, tokens = image_cache.shape[:2]
    part = stream.shape[1]
    chunks = part // LANES
    scale = 1.0 / math.sqrt(head)
    out_width = self_output.shape[1]
    shape = jax.ShapeDtypeStruct
    mig = migration.T
    my_row = lax.axis_index("rows").astype(i32)[None]
    my_column = lax.axis_index("heads").astype(i32)[None]

    packed = pl.pallas_call(
        functools.partial(pack_body, rows),
        out_shape=shape((devices, rows, width + LANES), bf16),
        in_specs=[smem(), vmem()],
        out_specs=vmem(),
        name="pack",
    )(mig, cross_query)
    asked = lax.all_to_all(packed, "rows", 0, 0, tiled=True).reshape(everyone, width + LANES)

    early_len = history // 4
    early, late, attended = pl.pallas_call(
        functools.partial(own_body, rows, pages, page_len, scale),
        out_shape=(
            shape((devices * 2, early_len, both), bf16),
            shape((devices * 2, history - early_len, both), bf16),
            shape((rows * heads, head), bf16),
        ),
        in_specs=[smem(), smem(), smem(), anywhere(), vmem(), vmem()],
        out_specs=(anywhere(), anywhere(), vmem()),
        scratch_shapes=[
            VMEM((rows, history, both), bf16),
            VMEM((rows * heads, head), f32),
            pltpu.SemaphoreType.DMA((rows, pages)),
            pltpu.SemaphoreType.DMA((rows,)),
            pltpu.SemaphoreType.DMA((rows,)),
        ],
        cost_estimate=pl.CostEstimate(
            flops=4 * rows * heads * history * head,
            bytes_accessed=4 * rows * history * both,
            transcendentals=rows * heads * history,
        ),
        compiler_params=pltpu.CompilerParams(vmem_limit_bytes=61 << 20),
        name="own",
    )(
        page_table.T,
        lengths,
        mig,
        cache_pool.reshape(pool_pages, page_len, both),
        new_kv.reshape(rows, both),
        self_query,
    )

    message_width = width + 3 * LANES
    message = pl.pallas_call(
        functools.partial(cross_body, rows, scale),
        out_shape=shape((everyone, message_width), bf16),
        in_specs=[smem(), vmem(), vmem(), vmem(), vmem(), vmem()],
        out_specs=vmem(),
        scratch_shapes=[
            VMEM((everyone, width), bf16),
            VMEM((everyone, width + LANES), bf16),
            VMEM((rows * chunks, LANES), f32),
        ],
        cost_estimate=pl.CostEstimate(
            flops=4 * everyone * heads * tokens * head + 8 * everyone * everyone * width,
            bytes_accessed=2 * images * tokens * both + 4 * everyone * width,
            transcendentals=everyone * heads * tokens,
        ),
        compiler_params=pltpu.CompilerParams(vmem_limit_bytes=40 << 20),
        name="cross",
    )(
        mig,
        asked,
        image_of.reshape(1, everyone),
        image_cache.reshape(images, tokens, both),
        attended,
        stream,
    )
    came = lax.all_to_all(
        message.reshape(devices, rows, message_width), "rows", 0, 0, tiled=True
    )
    early, came = lax.optimization_barrier((early, came))
    early = lax.all_to_all(
        early.reshape(devices, 2 * early_len, both), "rows", 0, 0, tiled=True
    )

    slot_attended, slot_cross, slot_stream, source = pl.pallas_call(
        functools.partial(settle_body, rows),
        out_shape=(
            shape((rows, width), bf16),
            shape((rows, width), bf16),
            shape((rows, part), bf16),
            shape((8, LANES), i32),
        ),
        in_specs=[smem(), vmem(), vmem()],
        out_specs=(vmem(), vmem(), vmem(), vmem()),
        scratch_shapes=[VMEM((devices, rows, LANES), f32)],
        cost_estimate=pl.CostEstimate(
            flops=4 * everyone * width,
            bytes_accessed=4 * everyone * width,
            transcendentals=everyone * LANES,
        ),
        compiler_params=pltpu.CompilerParams(vmem_limit_bytes=52 << 20),
        name="combine",
    )(my_row, asked, came)

    parts = pl.pallas_call(
        project_body,
        grid_spec=pltpu.PrefetchScalarGridSpec(
            num_scalar_prefetch=1,
            grid=(columns,),
            in_specs=[
                pl.BlockSpec((rows, width), lambda o, me: (0, 0)),
                pl.BlockSpec((rows, width), lambda o, me: (0, 0)),
                pl.BlockSpec((width, part), lambda o, me: (0, lax.rem(me[0] + o, columns))),
                pl.BlockSpec((width, part), lambda o, me: (0, lax.rem(me[0] + o, columns))),
            ],
            out_specs=pl.BlockSpec((1, 2 * rows, part), lambda o, me: (o, 0, 0)),
        ),
        out_shape=shape((columns, 2 * rows, part), f32),
        cost_estimate=pl.CostEstimate(
            flops=4 * rows * width * out_width,
            bytes_accessed=4 * width * out_width,
            transcendentals=0,
        ),
        compiler_params=pltpu.CompilerParams(vmem_limit_bytes=52 << 20),
        name="project",
    )(my_column, slot_attended, slot_cross, self_output, cross_output)
    summed = parts[0]
    for o in range(1, columns):
        summed = summed + lax.ppermute(
            parts[o], "heads", [(c, (c + o) % columns) for c in range(columns)]
        )
    self_update = (slot_stream.astype(f32) + summed[:rows]).astype(bf16)
    cross_update = (jnp.tanh(cross_gate[0]) * summed[rows:]).astype(bf16)

    late, early, self_update, cross_update = lax.optimization_barrier(
        (late, early, self_update, cross_update)
    )
    late = lax.all_to_all(
        late.reshape(devices, 2 * (history - early_len), both), "rows", 0, 0, tiled=True
    )
    new_cache = pl.pallas_call(
        place_body,
        in_specs=[smem(), anywhere(), anywhere()],
        out_specs=anywhere(),
        out_shape=shape((rows, history, both), bf16),
        scratch_shapes=[
            VMEM((rows, history, both), bf16),
            pltpu.SemaphoreType.DMA((rows,)),
            pltpu.SemaphoreType.DMA((rows,)),
            pltpu.SemaphoreType.DMA((rows,)),
        ],
        cost_estimate=pl.CostEstimate(
            flops=0, bytes_accessed=4 * rows * history * both, transcendentals=0
        ),
        name="place",
    )(
        source,
        early.reshape(devices * 2, early_len, both),
        late.reshape(devices * 2, history - early_len, both),
    )
    return (self_update, cross_update, new_cache.reshape(rows, history, 1, both))


def solution(mesh):
    in_specs = (
        P("rows", "heads"),
        P("rows", "heads"),
        P("rows", "heads", None),
        P("rows", None, "heads", None),
        P("rows", None),
        P("rows"),
        P("rows", None),
        P(),
        P("rows", "heads"),
        P(None, "rows", "heads", None),
        P("heads", None),
        P("heads", None),
        P(),
    )
    out_specs = (P("rows", "heads"), P("rows", "heads"), P("rows", None, "heads", None))
    return jax.shard_map(
        per_device, mesh=mesh, in_specs=in_specs, out_specs=out_specs, check_vma=False
    )
```

```python
import functools
import math

import jax
import jax.numpy as jnp
from jax import lax
from jax.experimental import pallas as pl
from jax.experimental.pallas import tpu as pltpu
from jax.sharding import PartitionSpec as P

very_low = -1e30
bf16 = jnp.bfloat16
f32 = jnp.float32
i32 = jnp.int32
LANES = 128
VMEM = pltpu.VMEM
SMEM = pltpu.SMEM


def vmem():
    return pl.BlockSpec(memory_space=VMEM)


def smem():
    return pl.BlockSpec(memory_space=SMEM)


def anywhere():
    return pl.BlockSpec(memory_space=pl.ANY)


def iota(shape, dim):
    return lax.broadcasted_iota(i32, shape, dim)


def onto(a, b):
    return lax.dot_general(a, b, (((0,), (0,)), ((), ())), preferred_element_type=f32)


def against(a, b):
    return lax.dot_general(a, b, (((1,), (1,)), ((), ())), preferred_element_type=f32)


def ranks_of(mig_ref, count):
    targets = [mig_ref[0, r] for r in range(count)]
    ranks = []
    for r in range(count):
        rank = jnp.int32(0)
        for e in range(r):
            rank = rank + (targets[e] == targets[r]).astype(i32)
        ranks.append(jnp.minimum(rank, 1))
    return targets, ranks


def pack_body(rows, mig_ref, query_ref, out_ref):
    targets, ranks = ranks_of(mig_ref, rows)
    width = query_ref.shape[1]
    sub, lane = iota((rows, LANES), 0), iota((rows, LANES), 1)
    about = jnp.full((rows, LANES), -1, i32)
    for r in range(rows):
        slot = jnp.where(targets[r] >= 0, targets[r] * rows + mig_ref[1, r], -1)
        about = jnp.where((sub == r) & (lane == 0), slot, about)
        about = jnp.where((sub == r) & (lane == 1), ranks[r], about)
    about = about.astype(f32).astype(bf16)
    for d in range(out_ref.shape[0]):
        out_ref[d, :, 0:width] = query_ref[...]
        out_ref[d, :, width : width + LANES] = about


def own_body(
    rows, pages, page_len, scale, side, pt_ref, len_ref, mig_ref, me_ref, pool, kv_ref, query_ref,
    *refs,
):
    across, down, (att_ref, held, split_ref, in_sem, across_sem, down_sem) = (
        refs[:side],
        refs[side : 2 * side],
        refs[2 * side :],
    )
    targets, ranks = ranks_of(mig_ref, rows)
    history = pages * page_len
    half = history // 2
    head = kv_ref.shape[1] // 2
    heads = query_ref.shape[1] // head
    my_z, my_x = me_ref[0] // side, me_ref[0] % side

    def fetching(r, p):
        return pltpu.make_async_copy(
            pool.at[pt_ref[p, r]], held.at[r, pl.ds(p * page_len, page_len)], in_sem.at[r, p]
        )

    def send(r):
        to_z, to_x = targets[r] // side, targets[r] % side
        shift_x, shift_z = (to_x - my_x) & (side - 1), (to_z - my_z) & (side - 1)
        live = targets[r] >= 0
        for n in range(side):

            @pl.when(live & (shift_x == n))
            def _():
                pltpu.make_async_copy(
                    held.at[r, pl.ds(0, half)], across[n].at[to_z * 2 + ranks[r]], across_sem.at[r]
                ).start()

            @pl.when(live & (shift_z == n))
            def _():
                pltpu.make_async_copy(
                    held.at[r, pl.ds(half, half)], down[n].at[to_x * 2 + ranks[r]], down_sem.at[r]
                ).start()

    for r in range(rows):
        for p in range(pages):
            fetching(r, p).start()
    for h in range(heads):
        split_ref[pl.ds(h, rows, stride=heads), :] = query_ref[:, h * head : (h + 1) * head].astype(
            f32
        )
    for r in range(rows):
        for p in range(pages):
            fetching(r, p).wait()
        length = len_ref[r]
        base = pl.multiple_of((length // 16) * 16, 16)
        block = held[r, pl.ds(base, 16), :].astype(f32)
        token = kv_ref[r : r + 1, :].astype(f32)
        here = iota(block.shape, 0) == length - base
        held[r, pl.ds(base, 16), :] = jnp.where(here, token, block).astype(bf16)

        send(r)

    for r in range(rows):
        queries = split_ref[r * heads : (r + 1) * heads, :].astype(bf16)
        scores = against(queries, held[r, :, 0:head]) * scale
        scores = jnp.where(iota((heads, history), 1) <= len_ref[r], scores, very_low)
        weights = jnp.exp(scores - jnp.max(scores, axis=1, keepdims=True))
        total = jnp.sum(weights, axis=1, keepdims=True)
        blended = jnp.dot(weights.astype(bf16), held[r, :, head:], preferred_element_type=f32)
        att_ref[r * heads : (r + 1) * heads, :] = (blended / total).astype(bf16)

    for r in range(rows):

        @pl.when(targets[r] >= 0)
        def _():
            pltpu.make_async_copy(
                held.at[r, pl.ds(0, half)], across[0].at[0], across_sem.at[r]
            ).wait()
            pltpu.make_async_copy(
                held.at[r, pl.ds(half, half)], down[0].at[0], down_sem.at[r]
            ).wait()


def cross_body(
    rows, scale, mig_ref, asked_ref, image_row_ref, cache_ref, att_ref, stream_ref, out_ref,
    sorted_ref, part_ref, split_ref,
):
    images, tokens, both = cache_ref.shape
    head = both // 2
    everyone = asked_ref.shape[0]
    width = asked_ref.shape[1] - LANES
    heads = width // head
    group = everyone // images
    square = (everyone, everyone)
    image_row = image_row_ref[...]
    diagonal = iota(square, 1) == iota(square, 0)
    image_col = jnp.sum(
        jnp.where(diagonal, image_row.astype(f32), 0.0), axis=1, keepdims=True
    ).astype(i32)
    same = (image_col == image_row) & (iota(square, 1) < iota(square, 0))
    rank = jnp.sum(jnp.where(same, 1.0, 0.0), axis=1, keepdims=True).astype(i32)
    by_image = (iota(square, 1) == image_col * group + rank).astype(f32).astype(bf16)
    slot = asked_ref[:, width : width + 1].astype(f32).astype(i32)
    by_slot = (iota(square, 1) == slot).astype(f32).astype(bf16)
    sorted_ref[...] = onto(by_image, asked_ref[:, 0:width]).astype(bf16)
    order = onto(by_slot, by_image).astype(bf16)
    stacked = heads * group
    lane = iota((stacked, LANES), 1)
    head_of = iota((stacked, LANES), 0) // group
    for i in range(images):
        at = slice(i * group, (i + 1) * group)
        queries = jnp.concatenate(
            [sorted_ref[at, h * head : (h + 1) * head] for h in range(heads)], axis=0
        )
        scores = against(queries, cache_ref[i, :, 0:head]) * scale
        top = jnp.max(scores, axis=1, keepdims=True)
        top_hi = top.astype(bf16).astype(f32)
        top_lo = (top - top_hi).astype(bf16).astype(f32)
        weights = jnp.exp(scores - (top_hi + top_lo))
        total = jnp.sum(weights, axis=1, keepdims=True)
        total_hi = total.astype(bf16).astype(f32)
        total_lo = (total - total_hi).astype(bf16).astype(f32)
        blended = jnp.dot(weights.astype(bf16), cache_ref[i, :, head:], preferred_element_type=f32)
        blended = (blended / total).astype(bf16)
        about = jnp.zeros((stacked, LANES), f32)
        for n, stat in enumerate((top_hi, top_lo, total_hi, total_lo)):
            about = jnp.where(lane == n * heads + head_of, stat, about)
        packed = about[0:group]
        for h in range(1, heads):
            packed = packed + about[h * group : (h + 1) * group]
        for h in range(heads):
            part_ref[at, h * head : (h + 1) * head] = blended[h * group : (h + 1) * group]
        part_ref[at, width : width + LANES] = packed.astype(bf16)
    out_ref[:, 0 : width + LANES] = jnp.dot(
        order, part_ref[...], preferred_element_type=f32
    ).astype(bf16)
    targets, ranks = ranks_of(mig_ref, rows)
    chunks = stream_ref.shape[1] // LANES
    for c in range(chunks):
        split_ref[pl.ds(c, rows, stride=chunks), :] = stream_ref[
            :, c * LANES : (c + 1) * LANES
        ].astype(f32)
    lane_a = iota((1, rows * heads), 1)
    lane_s = iota((1, rows * chunks), 1)
    to_a = jnp.full(lane_a.shape, -1, i32)
    to_s = jnp.full(lane_s.shape, -1, i32)
    for r in range(rows):
        live = targets[r] >= 0
        base_a = jnp.where(live, targets[r] * rows + ranks[r] * heads, -rows * 64)
        base_s = jnp.where(live, targets[r] * rows + ranks[r] * chunks, -rows * 64)
        to_a = jnp.where(lane_a // heads == r, base_a + lane_a % heads, to_a)
        to_s = jnp.where(lane_s // chunks == r, base_s + lane_s % chunks, to_s)
    pick_a = (iota((everyone, rows * heads), 0) == to_a).astype(f32).astype(bf16)
    pick_s = (iota((everyone, rows * chunks), 0) == to_s).astype(f32).astype(bf16)
    at = width + LANES
    out_ref[:, at : at + LANES] = jnp.dot(
        pick_a, att_ref[...], preferred_element_type=f32
    ).astype(bf16)
    out_ref[:, at + LANES : at + 2 * LANES] = jnp.dot(
        pick_s, split_ref[...].astype(bf16), preferred_element_type=f32
    ).astype(bf16)


def settle_body(
    rows, me_ref, asked_ref, came_ref, att_ref, cross_ref, stream_ref, source_ref, coef_ref
):
    sources = came_ref.shape[0]
    everyone = asked_ref.shape[0]
    width = asked_ref.shape[1] - LANES
    heads = width // LANES
    chunks = stream_ref.shape[1] // LANES
    tall = (everyone, LANES)
    slot = asked_ref[:, width : width + 1].astype(f32).astype(i32)
    rank = asked_ref[:, width + 1 : width + 2].astype(f32).astype(i32)
    lane = iota(tall, 1)
    source = iota(tall, 0) // rows
    match = ((slot - me_ref[0] * rows == lane) & (lane < rows)).astype(f32).astype(bf16)
    facts = jnp.where(lane == 0, source * 2 + rank, 0)
    facts = jnp.where(lane == 1, source * rows + rank * heads, facts)
    facts = jnp.where(lane == 2, source * rows + rank * chunks, facts)
    facts = jnp.where(lane == 3, 1, facts).astype(f32).astype(bf16)
    by_lane = onto(facts, match)
    source_ref[...] = jnp.where(by_lane[3:4] > 0.5, by_lane[0:1], -1.0).astype(i32) + jnp.zeros(
        source_ref.shape, i32
    )
    by_row = onto(match, facts)[0:rows]
    live = by_row[:, 3:4] > 0.5
    base_a = jnp.where(live, by_row[:, 1:2], -4096.0).astype(i32)
    base_s = jnp.where(live, by_row[:, 2:3], -4096.0).astype(i32)
    column = iota((rows, everyone), 1)
    at = width + LANES
    own_a = came_ref[:, :, at : at + LANES].reshape(everyone, LANES)
    own_s = came_ref[:, :, at + LANES : at + 2 * LANES].reshape(everyone, LANES)
    for h in range(heads):
        pick = (column == base_a + h).astype(f32).astype(bf16)
        att_ref[:, h * LANES : (h + 1) * LANES] = jnp.dot(
            pick, own_a, preferred_element_type=f32
        ).astype(bf16)
    for c in range(chunks):
        pick = (column == base_s + c).astype(f32).astype(bf16)
        stream_ref[:, c * LANES : (c + 1) * LANES] = jnp.dot(
            pick, own_s, preferred_element_type=f32
        ).astype(bf16)
    highest = None
    for s in range(sources):
        about = came_ref[s, :, width : width + LANES].astype(f32)
        about = about + pltpu.roll(about, LANES - heads, 1)
        coef_ref[s] = about
        highest = about if s == 0 else jnp.maximum(highest, about)
    total = jnp.zeros((rows, LANES), f32)
    for s in range(sources):
        about = coef_ref[s]
        share = jnp.exp(about - highest) * pltpu.roll(about, LANES - 2 * heads, 1)
        coef_ref[s] = share
        total = total + share
    over = jnp.where(live, 1.0 / total, 0.0)
    for h in range(heads):
        blended = jnp.zeros((rows, LANES), f32)
        for s in range(sources):
            part = came_ref[s, :, h * LANES : (h + 1) * LANES].astype(f32)
            blended = blended + coef_ref[s][:, h : h + 1] * part
        blended = jnp.where(live, blended * over[:, h : h + 1], 0.0)
        cross_ref[:, h * LANES : (h + 1) * LANES] = blended.astype(bf16)


def project_body(me_ref, att_ref, cross_ref, self_w_ref, cross_w_ref, out_ref):
    rows = att_ref.shape[0]
    out_ref[0, 0:rows] = jnp.dot(att_ref[...], self_w_ref[...], preferred_element_type=f32)
    out_ref[0, rows : 2 * rows] = jnp.dot(
        cross_ref[...], cross_w_ref[...], preferred_element_type=f32
    )


def mix_body(side, me_ref, *refs):
    sent_x, sent_z = refs[:side], refs[side : 2 * side]
    next_z, next_x = refs[2 * side : 3 * side - 1], refs[3 * side - 1 : 4 * side - 2]
    held, in_sem, out_sem = refs[4 * side - 2 :]
    mine = me_ref[0] // side, me_ref[0] % side
    moves = []
    for here, came, onward in ((mine[0], sent_x, next_z), (mine[1], sent_z, next_x)):
        for shift in range(1, side):
            for n in range(side):
                at = ((here + shift) & (side - 1)) * 2
                moves.append((came[n].at[pl.ds(at, 2)], onward[shift - 1].at[pl.ds(2 * n, 2)]))
    for n, (source, _) in enumerate(moves):
        pltpu.make_async_copy(source, held.at[n], in_sem.at[n]).start()
    for n, (source, target) in enumerate(moves):
        pltpu.make_async_copy(source, held.at[n], in_sem.at[n]).wait()
        pltpu.make_async_copy(held.at[n], target, out_sem.at[n]).start()
    for n, (_, target) in enumerate(moves):
        pltpu.make_async_copy(held.at[n], target, out_sem.at[n]).wait()


def place_body(side, source_ref, me_ref, *refs):
    near_x, far_z = refs[:side], refs[side : 2 * side - 1]
    near_z, far_x = refs[2 * side - 1 : 3 * side - 1], refs[3 * side - 1 : 4 * side - 2]
    out, held, first_sem, last_sem, out_sem = refs[4 * side - 2 :]
    rows, history, _ = held.shape
    half = history // 2
    my_z, my_x = me_ref[0] // side, me_ref[0] % side

    def fetch(ref, at, t, begin, sem):
        return pltpu.make_async_copy(ref.at[at], held.at[t, pl.ds(begin, half)], sem.at[t])

    def begin(t, carry):
        code = source_ref[0, t]
        live = code >= 0
        code = jnp.maximum(code, 0)
        source, rank = code // 2, code % 2
        shift_z = (my_z - source // side) & (side - 1)
        shift_x = (my_x - source % side) & (side - 1)
        for n in range(side):

            @pl.when(live & (shift_z == 0) & (shift_x == n))
            def _():
                fetch(near_x[n], my_z * 2 + rank, t, 0, first_sem).start()

            @pl.when(live & (shift_x == 0) & (shift_z == n))
            def _():
                fetch(near_z[n], my_x * 2 + rank, t, half, last_sem).start()

        for n in range(1, side):

            @pl.when(live & (shift_z == n))
            def _():
                fetch(far_z[n - 1], shift_x * 2 + rank, t, 0, first_sem).start()

            @pl.when(live & (shift_x == n))
            def _():
                fetch(far_x[n - 1], shift_z * 2 + rank, t, half, last_sem).start()

        @pl.when(jnp.logical_not(live))
        def _():
            held[t] = jnp.zeros(held.shape[1:], bf16)

        return carry

    def finish(t, carry):
        @pl.when(source_ref[0, t] >= 0)
        def _():
            fetch(near_x[0], 0, t, 0, first_sem).wait()
            fetch(near_z[0], 0, t, half, last_sem).wait()

        pltpu.make_async_copy(held.at[t], out.at[t], out_sem.at[t]).start()
        return carry

    lax.fori_loop(0, rows, begin, 0)
    lax.fori_loop(0, rows, finish, 0)
    for t in range(rows):
        pltpu.make_async_copy(held.at[t], out.at[t], out_sem.at[t]).wait()


def in_order(found, shifts):
    return [found[0]] + [found[1 + shifts.index(n)] for n in range(1, len(found))]


def per_device(
    stream,
    self_query,
    new_kv,
    cache_pool,
    page_table,
    lengths,
    migration,
    image_of,
    cross_query,
    image_cache,
    self_output,
    cross_output,
    cross_gate,
):
    rows, width = cross_query.shape
    devices = lax.axis_size("rows")
    columns = lax.axis_size("heads")
    everyone = rows * devices
    pages = page_table.shape[1]
    pool_pages, page_len, _, both = cache_pool.shape
    head = both // 2
    heads = width // head
    history = pages * page_len
    images, tokens = image_cache.shape[:2]
    part = stream.shape[1]
    chunks = part // LANES
    scale = 1.0 / math.sqrt(head)
    out_width = self_output.shape[1]
    shape = jax.ShapeDtypeStruct
    mig = migration.T
    my_row = lax.axis_index("rows").astype(i32)[None]
    my_column = lax.axis_index("heads").astype(i32)[None]

    packed = pl.pallas_call(
        functools.partial(pack_body, rows),
        out_shape=shape((devices, rows, width + LANES), bf16),
        in_specs=[smem(), vmem()],
        out_specs=vmem(),
        name="pack",
    )(mig, cross_query)
    asked = lax.all_to_all(packed, "rows", 0, 0, tiled=True).reshape(everyone, width + LANES)

    side = math.isqrt(devices)
    shifts = (1, *range(side - 1, 1, -1))
    half = history // 2
    bucket = shape((2 * side, half, both), bf16)
    *buckets, attended = pl.pallas_call(
        functools.partial(own_body, rows, pages, page_len, scale, side),
        out_shape=(*([bucket] * (2 * side)), shape((rows * heads, head), bf16)),
        in_specs=[smem(), smem(), smem(), smem(), anywhere(), vmem(), vmem()],
        out_specs=(*([anywhere()] * (2 * side)), vmem()),
        scratch_shapes=[
            VMEM((rows, history, both), bf16),
            VMEM((rows * heads, head), f32),
            pltpu.SemaphoreType.DMA((rows, pages)),
            pltpu.SemaphoreType.DMA((rows,)),
            pltpu.SemaphoreType.DMA((rows,)),
        ],
        cost_estimate=pl.CostEstimate(
            flops=4 * rows * heads * history * head,
            bytes_accessed=4 * rows * history * both,
            transcendentals=rows * heads * history,
        ),
        compiler_params=pltpu.CompilerParams(vmem_limit_bytes=61 << 20),
        name="own",
    )(
        page_table.T,
        lengths,
        mig,
        my_row,
        cache_pool.reshape(pool_pages, page_len, both),
        new_kv.reshape(rows, both),
        self_query,
    )

    def along(dz, dx):
        return [
            (z * side + x, ((z + dz) % side) * side + (x + dx) % side)
            for z in range(side)
            for x in range(side)
        ]

    near_x, near_z = [buckets[0]], [buckets[side]]
    for n in shifts:
        near_x.append(lax.ppermute(buckets[n], "rows", along(0, n)))
        near_z.append(lax.ppermute(buckets[side + n], "rows", along(n, 0)))
    near_x, near_z = in_order(near_x, shifts), in_order(near_z, shifts)

    message_width = width + 3 * LANES
    message = pl.pallas_call(
        functools.partial(cross_body, rows, scale),
        out_shape=shape((everyone, message_width), bf16),
        in_specs=[smem(), vmem(), vmem(), vmem(), vmem(), vmem()],
        out_specs=vmem(),
        scratch_shapes=[
            VMEM((everyone, width), bf16),
            VMEM((everyone, width + LANES), bf16),
            VMEM((rows * chunks, LANES), f32),
        ],
        cost_estimate=pl.CostEstimate(
            flops=4 * everyone * heads * tokens * head + 8 * everyone * everyone * width,
            bytes_accessed=2 * images * tokens * both + 4 * everyone * width,
            transcendentals=everyone * heads * tokens,
        ),
        compiler_params=pltpu.CompilerParams(vmem_limit_bytes=40 << 20),
        name="cross",
    )(
        mig,
        asked,
        image_of.reshape(1, everyone),
        image_cache.reshape(images, tokens, both),
        attended,
        stream,
    )
    came = lax.all_to_all(
        message.reshape(devices, rows, message_width), "rows", 0, 0, tiled=True
    )
    onward = pl.pallas_call(
        functools.partial(mix_body, side),
        out_shape=[bucket] * (2 * side - 2),
        in_specs=[smem()] + [anywhere()] * (2 * side),
        out_specs=[anywhere()] * (2 * side - 2),
        scratch_shapes=[
            VMEM((2 * side * (side - 1), 2, half, both), bf16),
            pltpu.SemaphoreType.DMA((2 * side * (side - 1),)),
            pltpu.SemaphoreType.DMA((2 * side * (side - 1),)),
        ],
        cost_estimate=pl.CostEstimate(
            flops=0, bytes_accessed=8 * rows * history * both, transcendentals=0
        ),
        name="mix",
    )(my_row, *near_x, *near_z)
    far_z, far_x = [None], [None]
    for n in shifts:
        far_z.append(lax.ppermute(onward[n - 1], "rows", along(n, 0)))
        far_x.append(lax.ppermute(onward[side - 1 + n - 1], "rows", along(0, n)))
    far_z, far_x = in_order(far_z, shifts)[1:], in_order(far_x, shifts)[1:]

    slot_attended, slot_cross, slot_stream, source = pl.pallas_call(
        functools.partial(settle_body, rows),
        out_shape=(
            shape((rows, width), bf16),
            shape((rows, width), bf16),
            shape((rows, part), bf16),
            shape((8, LANES), i32),
        ),
        in_specs=[smem(), vmem(), vmem()],
        out_specs=(vmem(), vmem(), vmem(), vmem()),
        scratch_shapes=[VMEM((devices, rows, LANES), f32)],
        cost_estimate=pl.CostEstimate(
            flops=4 * everyone * width,
            bytes_accessed=4 * everyone * width,
            transcendentals=everyone * LANES,
        ),
        compiler_params=pltpu.CompilerParams(vmem_limit_bytes=52 << 20),
        name="combine",
    )(my_row, asked, came)

    parts = pl.pallas_call(
        project_body,
        grid_spec=pltpu.PrefetchScalarGridSpec(
            num_scalar_prefetch=1,
            grid=(columns,),
            in_specs=[
                pl.BlockSpec((rows, width), lambda o, me: (0, 0)),
                pl.BlockSpec((rows, width), lambda o, me: (0, 0)),
                pl.BlockSpec((width, part), lambda o, me: (0, lax.rem(me[0] + o, columns))),
                pl.BlockSpec((width, part), lambda o, me: (0, lax.rem(me[0] + o, columns))),
            ],
            out_specs=pl.BlockSpec((1, 2 * rows, part), lambda o, me: (o, 0, 0)),
        ),
        out_shape=shape((columns, 2 * rows, part), f32),
        cost_estimate=pl.CostEstimate(
            flops=4 * rows * width * out_width,
            bytes_accessed=4 * width * out_width,
            transcendentals=0,
        ),
        compiler_params=pltpu.CompilerParams(vmem_limit_bytes=52 << 20),
        name="project",
    )(my_column, slot_attended, slot_cross, self_output, cross_output)
    summed = parts[0]
    for o in range(1, columns):
        summed = summed + lax.ppermute(
            parts[o], "heads", [(c, (c + o) % columns) for c in range(columns)]
        )
    self_update = (slot_stream.astype(f32) + summed[:rows]).astype(bf16)
    cross_update = (jnp.tanh(cross_gate[0]) * summed[rows:]).astype(bf16)

    new_cache = pl.pallas_call(
        functools.partial(place_body, side),
        in_specs=[smem(), smem()] + [anywhere()] * (4 * side - 2),
        out_specs=anywhere(),
        out_shape=shape((rows, history, both), bf16),
        scratch_shapes=[
            VMEM((rows, history, both), bf16),
            pltpu.SemaphoreType.DMA((rows,)),
            pltpu.SemaphoreType.DMA((rows,)),
            pltpu.SemaphoreType.DMA((rows,)),
        ],
        cost_estimate=pl.CostEstimate(
            flops=0, bytes_accessed=4 * rows * history * both, transcendentals=0
        ),
        name="place",
    )(source, my_row, *near_x, *far_z, *near_z, *far_x)
    return (self_update, cross_update, new_cache.reshape(rows, history, 1, both))


def solution(mesh):
    in_specs = (
        P("rows", "heads"),
        P("rows", "heads"),
        P("rows", "heads", None),
        P("rows", None, "heads", None),
        P("rows", None),
        P("rows"),
        P("rows", None),
        P(),
        P("rows", "heads"),
        P(None, "rows", "heads", None),
        P("heads", None),
        P("heads", None),
        P(),
    )
    out_specs = (P("rows", "heads"), P("rows", "heads"), P("rows", None, "heads", None))
    return jax.shard_map(
        per_device, mesh=mesh, in_specs=in_specs, out_specs=out_specs, check_vma=False
    )
```

```python
import functools
import math

import jax
import jax.numpy as jnp
from jax import lax
from jax.experimental import pallas as pl
from jax.experimental.pallas import tpu as pltpu
from jax.sharding import PartitionSpec as P

very_low = -1e30
bf16 = jnp.bfloat16
f32 = jnp.float32
i32 = jnp.int32
LANES = 128
VMEM = pltpu.VMEM
SMEM = pltpu.SMEM


def vmem():
    return pl.BlockSpec(memory_space=VMEM)


def smem():
    return pl.BlockSpec(memory_space=SMEM)


def anywhere():
    return pl.BlockSpec(memory_space=pl.ANY)


def iota(shape, dim):
    return lax.broadcasted_iota(i32, shape, dim)


def onto(a, b):
    return lax.dot_general(a, b, (((0,), (0,)), ((), ())), preferred_element_type=f32)


def against(a, b):
    return lax.dot_general(a, b, (((1,), (1,)), ((), ())), preferred_element_type=f32)


def ranks_of(mig_ref, count):
    targets = [mig_ref[0, r] for r in range(count)]
    ranks = []
    for r in range(count):
        rank = jnp.int32(0)
        for e in range(r):
            rank = rank + (targets[e] == targets[r]).astype(i32)
        ranks.append(jnp.minimum(rank, 1))
    return targets, ranks


def pack_body(rows, mig_ref, query_ref, out_ref):
    targets, ranks = ranks_of(mig_ref, rows)
    width = query_ref.shape[1]
    sub, lane = iota((rows, LANES), 0), iota((rows, LANES), 1)
    about = jnp.full((rows, LANES), -1, i32)
    for r in range(rows):
        slot = jnp.where(targets[r] >= 0, targets[r] * rows + mig_ref[1, r], -1)
        about = jnp.where((sub == r) & (lane == 0), slot, about)
        about = jnp.where((sub == r) & (lane == 1), ranks[r], about)
    about = about.astype(f32).astype(bf16)
    for d in range(out_ref.shape[0]):
        out_ref[d, :, 0:width] = query_ref[...]
        out_ref[d, :, width : width + LANES] = about


def own_body(
    rows, pages, page_len, side, pt_ref, len_ref, mig_ref, me_ref, pool, kv_ref, *refs,
):
    across, down, (whole, held, in_sem, across_sem, down_sem, whole_sem) = (
        refs[:side],
        refs[side : 2 * side],
        refs[2 * side :],
    )
    targets, ranks = ranks_of(mig_ref, rows)
    history = pages * page_len
    half = history // 2
    my_z, my_x = me_ref[0] // side, me_ref[0] % side

    def fetching(r, p):
        return pltpu.make_async_copy(
            pool.at[pt_ref[p, r]], held.at[r, pl.ds(p * page_len, page_len)], in_sem.at[r, p]
        )

    def send(r):
        to_z, to_x = targets[r] // side, targets[r] % side
        shift_x, shift_z = (to_x - my_x) & (side - 1), (to_z - my_z) & (side - 1)
        live = targets[r] >= 0
        for n in range(side):

            @pl.when(live & (shift_x == n))
            def _():
                pltpu.make_async_copy(
                    held.at[r, pl.ds(0, half)], across[n].at[to_z * 2 + ranks[r]], across_sem.at[r]
                ).start()

            @pl.when(live & (shift_z == n))
            def _():
                pltpu.make_async_copy(
                    held.at[r, pl.ds(half, half)], down[n].at[to_x * 2 + ranks[r]], down_sem.at[r]
                ).start()

    for r in range(rows):
        for p in range(pages):
            fetching(r, p).start()
    for r in range(rows):
        for p in range(pages):
            fetching(r, p).wait()
        length = len_ref[r]
        base = pl.multiple_of((length // 16) * 16, 16)
        block = held[r, pl.ds(base, 16), :].astype(f32)
        token = kv_ref[r : r + 1, :].astype(f32)
        here = iota(block.shape, 0) == length - base
        held[r, pl.ds(base, 16), :] = jnp.where(here, token, block).astype(bf16)

        send(r)
        pltpu.make_async_copy(held.at[r], whole.at[r], whole_sem.at[r]).start()

    for r in range(rows):
        pltpu.make_async_copy(held.at[r], whole.at[r], whole_sem.at[r]).wait()
    for r in range(rows):

        @pl.when(targets[r] >= 0)
        def _():
            pltpu.make_async_copy(
                held.at[r, pl.ds(0, half)], across[0].at[0], across_sem.at[r]
            ).wait()
            pltpu.make_async_copy(
                held.at[r, pl.ds(half, half)], down[0].at[0], down_sem.at[r]
            ).wait()


def self_body(rows, scale, len_ref, query_ref, whole_ref, att_ref, split_ref):
    _, history, both = whole_ref.shape
    head = both // 2
    heads = query_ref.shape[1] // head
    for h in range(heads):
        split_ref[pl.ds(h, rows, stride=heads), :] = query_ref[:, h * head : (h + 1) * head].astype(
            f32
        )
    for r in range(rows):
        queries = split_ref[r * heads : (r + 1) * heads, :].astype(bf16)
        scores = against(queries, whole_ref[r, :, 0:head]) * scale
        scores = jnp.where(iota((heads, history), 1) <= len_ref[r], scores, very_low)
        weights = jnp.exp(scores - jnp.max(scores, axis=1, keepdims=True))
        total = jnp.sum(weights, axis=1, keepdims=True)
        blended = jnp.dot(weights.astype(bf16), whole_ref[r, :, head:], preferred_element_type=f32)
        att_ref[r * heads : (r + 1) * heads, :] = (blended / total).astype(bf16)


def cross_body(
    rows, scale, mig_ref, asked_ref, image_row_ref, cache_ref, att_ref, stream_ref, out_ref,
    sorted_ref, part_ref, split_ref,
):
    images, _, both = cache_ref.shape
    head = both // 2
    everyone = asked_ref.shape[0]
    width = asked_ref.shape[1] - LANES
    heads = width // head
    group = everyone // images
    square = (everyone, everyone)
    image_row = image_row_ref[...]
    diagonal = iota(square, 1) == iota(square, 0)
    image_col = jnp.sum(
        jnp.where(diagonal, image_row.astype(f32), 0.0), axis=1, keepdims=True
    ).astype(i32)
    same = (image_col == image_row) & (iota(square, 1) < iota(square, 0))
    rank = jnp.sum(jnp.where(same, 1.0, 0.0), axis=1, keepdims=True).astype(i32)
    by_image = (iota(square, 1) == image_col * group + rank).astype(f32).astype(bf16)
    slot = asked_ref[:, width : width + 1].astype(f32).astype(i32)
    by_slot = (iota(square, 1) == slot).astype(f32).astype(bf16)
    sorted_ref[...] = onto(by_image, asked_ref[:, 0:width]).astype(bf16)
    order = onto(by_slot, by_image).astype(bf16)
    stacked = heads * group
    lane = iota((stacked, LANES), 1)
    head_of = iota((stacked, LANES), 0) // group
    for i in range(images):
        at = slice(i * group, (i + 1) * group)
        queries = jnp.concatenate(
            [sorted_ref[at, h * head : (h + 1) * head] for h in range(heads)], axis=0
        )
        scores = against(queries, cache_ref[i, :, 0:head]) * scale
        top = jnp.max(scores, axis=1, keepdims=True)
        top_hi = top.astype(bf16).astype(f32)
        top_lo = (top - top_hi).astype(bf16).astype(f32)
        weights = jnp.exp(scores - (top_hi + top_lo))
        total = jnp.sum(weights, axis=1, keepdims=True)
        total_hi = total.astype(bf16).astype(f32)
        total_lo = (total - total_hi).astype(bf16).astype(f32)
        blended = jnp.dot(weights.astype(bf16), cache_ref[i, :, head:], preferred_element_type=f32)
        blended = (blended / total).astype(bf16)
        about = jnp.zeros((stacked, LANES), f32)
        for n, stat in enumerate((top_hi, top_lo, total_hi, total_lo)):
            about = jnp.where(lane == n * heads + head_of, stat, about)
        packed = about[0:group]
        for h in range(1, heads):
            packed = packed + about[h * group : (h + 1) * group]
        for h in range(heads):
            part_ref[at, h * head : (h + 1) * head] = blended[h * group : (h + 1) * group]
        part_ref[at, width : width + LANES] = packed.astype(bf16)
    out_ref[:, 0 : width + LANES] = jnp.dot(
        order, part_ref[...], preferred_element_type=f32
    ).astype(bf16)
    targets, ranks = ranks_of(mig_ref, rows)
    chunks = stream_ref.shape[1] // LANES
    for c in range(chunks):
        split_ref[pl.ds(c, rows, stride=chunks), :] = stream_ref[
            :, c * LANES : (c + 1) * LANES
        ].astype(f32)
    lane_a = iota((1, rows * heads), 1)
    lane_s = iota((1, rows * chunks), 1)
    to_a = jnp.full(lane_a.shape, -1, i32)
    to_s = jnp.full(lane_s.shape, -1, i32)
    for r in range(rows):
        live = targets[r] >= 0
        base_a = jnp.where(live, targets[r] * rows + ranks[r] * heads, -rows * 64)
        base_s = jnp.where(live, targets[r] * rows + ranks[r] * chunks, -rows * 64)
        to_a = jnp.where(lane_a // heads == r, base_a + lane_a % heads, to_a)
        to_s = jnp.where(lane_s // chunks == r, base_s + lane_s % chunks, to_s)
    pick_a = (iota((everyone, rows * heads), 0) == to_a).astype(f32).astype(bf16)
    pick_s = (iota((everyone, rows * chunks), 0) == to_s).astype(f32).astype(bf16)
    at = width + LANES
    out_ref[:, at : at + LANES] = jnp.dot(
        pick_a, att_ref[...], preferred_element_type=f32
    ).astype(bf16)
    out_ref[:, at + LANES : at + 2 * LANES] = jnp.dot(
        pick_s, split_ref[...].astype(bf16), preferred_element_type=f32
    ).astype(bf16)


def settle_body(
    rows, me_ref, asked_ref, came_ref, att_ref, cross_ref, stream_ref, source_ref, coef_ref
):
    sources = came_ref.shape[0]
    everyone = asked_ref.shape[0]
    width = asked_ref.shape[1] - LANES
    heads = width // LANES
    chunks = stream_ref.shape[1] // LANES
    tall = (everyone, LANES)
    slot = asked_ref[:, width : width + 1].astype(f32).astype(i32)
    rank = asked_ref[:, width + 1 : width + 2].astype(f32).astype(i32)
    lane = iota(tall, 1)
    source = iota(tall, 0) // rows
    match = ((slot - me_ref[0] * rows == lane) & (lane < rows)).astype(f32).astype(bf16)
    facts = jnp.where(lane == 0, source * 2 + rank, 0)
    facts = jnp.where(lane == 1, source * rows + rank * heads, facts)
    facts = jnp.where(lane == 2, source * rows + rank * chunks, facts)
    facts = jnp.where(lane == 3, 1, facts).astype(f32).astype(bf16)
    by_lane = onto(facts, match)
    source_ref[...] = jnp.where(by_lane[3:4] > 0.5, by_lane[0:1], -1.0).astype(i32) + jnp.zeros(
        source_ref.shape, i32
    )
    by_row = onto(match, facts)[0:rows]
    live = by_row[:, 3:4] > 0.5
    base_a = jnp.where(live, by_row[:, 1:2], -4096.0).astype(i32)
    base_s = jnp.where(live, by_row[:, 2:3], -4096.0).astype(i32)
    column = iota((rows, everyone), 1)
    at = width + LANES
    own_a = came_ref[:, :, at : at + LANES].reshape(everyone, LANES)
    own_s = came_ref[:, :, at + LANES : at + 2 * LANES].reshape(everyone, LANES)
    for h in range(heads):
        pick = (column == base_a + h).astype(f32).astype(bf16)
        att_ref[:, h * LANES : (h + 1) * LANES] = jnp.dot(
            pick, own_a, preferred_element_type=f32
        ).astype(bf16)
    for c in range(chunks):
        pick = (column == base_s + c).astype(f32).astype(bf16)
        stream_ref[:, c * LANES : (c + 1) * LANES] = jnp.dot(
            pick, own_s, preferred_element_type=f32
        ).astype(bf16)
    highest = None
    for s in range(sources):
        about = came_ref[s, :, width : width + LANES].astype(f32)
        about = about + pltpu.roll(about, LANES - heads, 1)
        coef_ref[s] = about
        highest = about if s == 0 else jnp.maximum(highest, about)
    total = jnp.zeros((rows, LANES), f32)
    for s in range(sources):
        about = coef_ref[s]
        share = jnp.exp(about - highest) * pltpu.roll(about, LANES - 2 * heads, 1)
        coef_ref[s] = share
        total = total + share
    over = jnp.where(live, 1.0 / total, 0.0)
    for h in range(heads):
        blended = jnp.zeros((rows, LANES), f32)
        for s in range(sources):
            part = came_ref[s, :, h * LANES : (h + 1) * LANES].astype(f32)
            blended = blended + coef_ref[s][:, h : h + 1] * part
        blended = jnp.where(live, blended * over[:, h : h + 1], 0.0)
        cross_ref[:, h * LANES : (h + 1) * LANES] = blended.astype(bf16)


def project_body(me_ref, att_ref, cross_ref, self_w_ref, cross_w_ref, out_ref):
    rows = att_ref.shape[0]
    out_ref[0, 0:rows] = jnp.dot(att_ref[...], self_w_ref[...], preferred_element_type=f32)
    out_ref[0, rows : 2 * rows] = jnp.dot(
        cross_ref[...], cross_w_ref[...], preferred_element_type=f32
    )


def mix_body(side, me_ref, *refs):
    sent_x, sent_z = refs[:side], refs[side : 2 * side]
    next_z, next_x = refs[2 * side : 3 * side - 1], refs[3 * side - 1 : 4 * side - 2]
    held, in_sem, out_sem = refs[4 * side - 2 :]
    mine = me_ref[0] // side, me_ref[0] % side
    moves = []
    for here, came, onward in ((mine[0], sent_x, next_z), (mine[1], sent_z, next_x)):
        for shift in range(1, side):
            for n in range(side):
                at = ((here + shift) & (side - 1)) * 2
                moves.append((came[n].at[pl.ds(at, 2)], onward[shift - 1].at[pl.ds(2 * n, 2)]))
    for n, (source, _) in enumerate(moves):
        pltpu.make_async_copy(source, held.at[n], in_sem.at[n]).start()
    for n, (source, target) in enumerate(moves):
        pltpu.make_async_copy(source, held.at[n], in_sem.at[n]).wait()
        pltpu.make_async_copy(held.at[n], target, out_sem.at[n]).start()
    for n, (_, target) in enumerate(moves):
        pltpu.make_async_copy(held.at[n], target, out_sem.at[n]).wait()


def place_body(side, source_ref, me_ref, *refs):
    near_x, far_z = refs[:side], refs[side : 2 * side - 1]
    near_z, far_x = refs[2 * side - 1 : 3 * side - 1], refs[3 * side - 1 : 4 * side - 2]
    out, held, first_sem, last_sem, out_sem = refs[4 * side - 2 :]
    rows, history, _ = held.shape
    half = history // 2
    my_z, my_x = me_ref[0] // side, me_ref[0] % side

    def fetch(ref, at, t, begin, sem):
        return pltpu.make_async_copy(ref.at[at], held.at[t, pl.ds(begin, half)], sem.at[t])

    def begin(t, carry):
        code = source_ref[0, t]
        live = code >= 0
        code = jnp.maximum(code, 0)
        source, rank = code // 2, code % 2
        shift_z = (my_z - source // side) & (side - 1)
        shift_x = (my_x - source % side) & (side - 1)
        for n in range(side):

            @pl.when(live & (shift_z == 0) & (shift_x == n))
            def _():
                fetch(near_x[n], my_z * 2 + rank, t, 0, first_sem).start()

            @pl.when(live & (shift_x == 0) & (shift_z == n))
            def _():
                fetch(near_z[n], my_x * 2 + rank, t, half, last_sem).start()

        for n in range(1, side):

            @pl.when(live & (shift_z == n))
            def _():
                fetch(far_z[n - 1], shift_x * 2 + rank, t, 0, first_sem).start()

            @pl.when(live & (shift_x == n))
            def _():
                fetch(far_x[n - 1], shift_z * 2 + rank, t, half, last_sem).start()

        @pl.when(jnp.logical_not(live))
        def _():
            held[t] = jnp.zeros(held.shape[1:], bf16)

        return carry

    def finish(t, carry):
        @pl.when(source_ref[0, t] >= 0)
        def _():
            fetch(near_x[0], 0, t, 0, first_sem).wait()
            fetch(near_z[0], 0, t, half, last_sem).wait()

        pltpu.make_async_copy(held.at[t], out.at[t], out_sem.at[t]).start()
        return carry

    lax.fori_loop(0, rows, begin, 0)
    lax.fori_loop(0, rows, finish, 0)
    for t in range(rows):
        pltpu.make_async_copy(held.at[t], out.at[t], out_sem.at[t]).wait()


def in_order(found, shifts):
    return [found[0]] + [found[1 + shifts.index(n)] for n in range(1, len(found))]


def per_device(
    stream,
    self_query,
    new_kv,
    cache_pool,
    page_table,
    lengths,
    migration,
    image_of,
    cross_query,
    image_cache,
    self_output,
    cross_output,
    cross_gate,
):
    rows, width = cross_query.shape
    devices = lax.axis_size("rows")
    columns = lax.axis_size("heads")
    everyone = rows * devices
    pages = page_table.shape[1]
    pool_pages, page_len, _, both = cache_pool.shape
    head = both // 2
    heads = width // head
    history = pages * page_len
    images, tokens = image_cache.shape[:2]
    part = stream.shape[1]
    chunks = part // LANES
    scale = 1.0 / math.sqrt(head)
    out_width = self_output.shape[1]
    shape = jax.ShapeDtypeStruct
    mig = migration.T
    my_row = lax.axis_index("rows").astype(i32)[None]
    my_column = lax.axis_index("heads").astype(i32)[None]

    packed = pl.pallas_call(
        functools.partial(pack_body, rows),
        out_shape=shape((devices, rows, width + LANES), bf16),
        in_specs=[smem(), vmem()],
        out_specs=vmem(),
        name="pack",
    )(mig, cross_query)
    asked = lax.all_to_all(packed, "rows", 0, 0, tiled=True).reshape(everyone, width + LANES)

    side = math.isqrt(devices)
    shifts = (1, *range(side - 1, 1, -1))
    half = history // 2
    bucket = shape((2 * side, half, both), bf16)
    *buckets, whole = pl.pallas_call(
        functools.partial(own_body, rows, pages, page_len, side),
        out_shape=(*([bucket] * (2 * side)), shape((rows, history, both), bf16)),
        in_specs=[smem(), smem(), smem(), smem(), anywhere(), vmem()],
        out_specs=(*([anywhere()] * (2 * side)), anywhere()),
        scratch_shapes=[
            VMEM((rows, history, both), bf16),
            pltpu.SemaphoreType.DMA((rows, pages)),
            pltpu.SemaphoreType.DMA((rows,)),
            pltpu.SemaphoreType.DMA((rows,)),
            pltpu.SemaphoreType.DMA((rows,)),
        ],
        compiler_params=pltpu.CompilerParams(vmem_limit_bytes=61 << 20),
        cost_estimate=pl.CostEstimate(
            flops=0, bytes_accessed=6 * rows * history * both, transcendentals=0
        ),
        name="own",
    )(
        page_table.T,
        lengths,
        mig,
        my_row,
        cache_pool.reshape(pool_pages, page_len, both),
        new_kv.reshape(rows, both),
    )
    attended = pl.pallas_call(
        functools.partial(self_body, rows, scale),
        out_shape=shape((rows * heads, head), bf16),
        in_specs=[smem(), vmem(), vmem()],
        out_specs=vmem(),
        scratch_shapes=[VMEM((rows * heads, head), f32)],
        cost_estimate=pl.CostEstimate(
            flops=4 * rows * heads * history * head,
            bytes_accessed=2 * rows * history * both,
            transcendentals=rows * heads * history,
        ),
        name="attend",
    )(lengths, self_query, whole)

    def along(dz, dx):
        return [
            (z * side + x, ((z + dz) % side) * side + (x + dx) % side)
            for z in range(side)
            for x in range(side)
        ]

    near_x, near_z = [buckets[0]], [buckets[side]]
    for n in shifts:
        near_x.append(lax.ppermute(buckets[n], "rows", along(0, n)))
        near_z.append(lax.ppermute(buckets[side + n], "rows", along(n, 0)))
    near_x, near_z = in_order(near_x, shifts), in_order(near_z, shifts)

    message_width = width + 3 * LANES
    message = pl.pallas_call(
        functools.partial(cross_body, rows, scale),
        out_shape=shape((everyone, message_width), bf16),
        in_specs=[smem(), vmem(), vmem(), vmem(), vmem(), vmem()],
        out_specs=vmem(),
        scratch_shapes=[
            VMEM((everyone, width), bf16),
            VMEM((everyone, width + LANES), bf16),
            VMEM((rows * chunks, LANES), f32),
        ],
        cost_estimate=pl.CostEstimate(
            flops=4 * everyone * heads * tokens * head + 8 * everyone * everyone * width,
            bytes_accessed=2 * images * tokens * both + 4 * everyone * width,
            transcendentals=everyone * heads * tokens,
        ),
        compiler_params=pltpu.CompilerParams(vmem_limit_bytes=40 << 20),
        name="cross",
    )(
        mig,
        asked,
        image_of.reshape(1, everyone),
        image_cache.reshape(images, tokens, both),
        attended,
        stream,
    )
    came = lax.all_to_all(message.reshape(devices, rows, message_width), "rows", 0, 0, tiled=True)
    onward = pl.pallas_call(
        functools.partial(mix_body, side),
        out_shape=[bucket] * (2 * side - 2),
        in_specs=[smem()] + [anywhere()] * (2 * side),
        out_specs=[anywhere()] * (2 * side - 2),
        scratch_shapes=[
            VMEM((2 * side * (side - 1), 2, half, both), bf16),
            pltpu.SemaphoreType.DMA((2 * side * (side - 1),)),
            pltpu.SemaphoreType.DMA((2 * side * (side - 1),)),
        ],
        cost_estimate=pl.CostEstimate(
            flops=0, bytes_accessed=8 * rows * history * both, transcendentals=0
        ),
        name="mix",
    )(my_row, *near_x, *near_z)
    far_z, far_x = [None], [None]
    for n in shifts:
        far_z.append(lax.ppermute(onward[n - 1], "rows", along(n, 0)))
        far_x.append(lax.ppermute(onward[side - 1 + n - 1], "rows", along(0, n)))
    far_z, far_x = in_order(far_z, shifts)[1:], in_order(far_x, shifts)[1:]

    slot_attended, slot_cross, slot_stream, source = pl.pallas_call(
        functools.partial(settle_body, rows),
        out_shape=(
            shape((rows, width), bf16),
            shape((rows, width), bf16),
            shape((rows, part), bf16),
            shape((8, LANES), i32),
        ),
        in_specs=[smem(), vmem(), vmem()],
        out_specs=(vmem(), vmem(), vmem(), vmem()),
        scratch_shapes=[VMEM((devices, rows, LANES), f32)],
        cost_estimate=pl.CostEstimate(
            flops=4 * everyone * width,
            bytes_accessed=4 * everyone * width,
            transcendentals=everyone * LANES,
        ),
        compiler_params=pltpu.CompilerParams(vmem_limit_bytes=61 << 20),
        name="combine",
    )(my_row, asked, came)

    parts = pl.pallas_call(
        project_body,
        grid_spec=pltpu.PrefetchScalarGridSpec(
            num_scalar_prefetch=1,
            grid=(columns,),
            in_specs=[
                pl.BlockSpec((rows, width), lambda o, me: (0, 0)),
                pl.BlockSpec((rows, width), lambda o, me: (0, 0)),
                pl.BlockSpec((width, part), lambda o, me: (0, lax.rem(me[0] + o, columns))),
                pl.BlockSpec((width, part), lambda o, me: (0, lax.rem(me[0] + o, columns))),
            ],
            out_specs=pl.BlockSpec((1, 2 * rows, part), lambda o, me: (o, 0, 0)),
        ),
        out_shape=shape((columns, 2 * rows, part), f32),
        cost_estimate=pl.CostEstimate(
            flops=4 * rows * width * out_width,
            bytes_accessed=4 * width * out_width,
            transcendentals=0,
        ),
        compiler_params=pltpu.CompilerParams(vmem_limit_bytes=61 << 20),
        name="project",
    )(my_column, slot_attended, slot_cross, self_output, cross_output)
    summed = parts[0]
    for o in range(1, columns):
        summed = summed + lax.ppermute(
            parts[o], "heads", [(c, (c + o) % columns) for c in range(columns)]
        )
    self_update = (slot_stream.astype(f32) + summed[:rows]).astype(bf16)
    cross_update = (jnp.tanh(cross_gate[0]) * summed[rows:]).astype(bf16)

    new_cache = pl.pallas_call(
        functools.partial(place_body, side),
        in_specs=[smem(), smem()] + [anywhere()] * (4 * side - 2),
        out_specs=anywhere(),
        out_shape=shape((rows, history, both), bf16),
        scratch_shapes=[
            VMEM((rows, history, both), bf16),
            pltpu.SemaphoreType.DMA((rows,)),
            pltpu.SemaphoreType.DMA((rows,)),
            pltpu.SemaphoreType.DMA((rows,)),
        ],
        cost_estimate=pl.CostEstimate(
            flops=0, bytes_accessed=4 * rows * history * both, transcendentals=0
        ),
        name="place",
    )(source, my_row, *near_x, *far_z, *near_z, *far_x)
    return (self_update, cross_update, new_cache.reshape(rows, history, 1, both))


def solution(mesh):
    in_specs = (
        P("rows", "heads"),
        P("rows", "heads"),
        P("rows", "heads", None),
        P("rows", None, "heads", None),
        P("rows", None),
        P("rows"),
        P("rows", None),
        P(),
        P("rows", "heads"),
        P(None, "rows", "heads", None),
        P("heads", None),
        P("heads", None),
        P(),
    )
    out_specs = (P("rows", "heads"), P("rows", "heads"), P("rows", None, "heads", None))

    return jax.shard_map(
        per_device, mesh=mesh, in_specs=in_specs, out_specs=out_specs, check_vma=False
    )
```

```python
import functools
import math

import jax
import jax.numpy as jnp
from jax import lax
from jax.experimental import pallas as pl
from jax.experimental.pallas import tpu as pltpu
from jax.sharding import PartitionSpec as P

very_low = -1e30
bf16 = jnp.bfloat16
f32 = jnp.float32
i32 = jnp.int32
LANES = 128
VMEM = pltpu.VMEM
SMEM = pltpu.SMEM


def vmem():
    return pl.BlockSpec(memory_space=VMEM)


def smem():
    return pl.BlockSpec(memory_space=SMEM)


def anywhere():
    return pl.BlockSpec(memory_space=pl.ANY)


def iota(shape, dim):
    return lax.broadcasted_iota(i32, shape, dim)


def onto(a, b):
    return lax.dot_general(a, b, (((0,), (0,)), ((), ())), preferred_element_type=f32)


def against(a, b):
    return lax.dot_general(a, b, (((1,), (1,)), ((), ())), preferred_element_type=f32)


def ranks_of(mig_ref, count):
    targets = [mig_ref[0, r] for r in range(count)]
    ranks = []
    for r in range(count):
        rank = jnp.int32(0)
        for e in range(r):
            rank = rank + (targets[e] == targets[r]).astype(i32)
        ranks.append(jnp.minimum(rank, 1))
    return targets, ranks


def pack_body(rows, mig_ref, query_ref, out_ref):
    targets, ranks = ranks_of(mig_ref, rows)
    width = query_ref.shape[1]
    sub, lane = iota((rows, LANES), 0), iota((rows, LANES), 1)
    about = jnp.full((rows, LANES), -1, i32)
    for r in range(rows):
        slot = jnp.where(targets[r] >= 0, targets[r] * rows + mig_ref[1, r], -1)
        about = jnp.where((sub == r) & (lane == 0), slot, about)
        about = jnp.where((sub == r) & (lane == 1), ranks[r], about)
    about = about.astype(f32).astype(bf16)
    for d in range(out_ref.shape[0]):
        out_ref[d, :, 0:width] = query_ref[...]
        out_ref[d, :, width : width + LANES] = about


def own_body(
    rows, pages, page_len, side, pt_ref, len_ref, mig_ref, me_ref, pool, kv_ref, *refs,
):
    across, down, (whole, held, in_sem, across_sem, down_sem, whole_sem) = (
        refs[:side],
        refs[side : 2 * side],
        refs[2 * side :],
    )
    targets, ranks = ranks_of(mig_ref, rows)
    history = pages * page_len
    half = history // 2
    my_z, my_x = me_ref[0] // side, me_ref[0] % side

    def fetching(r, p):
        return pltpu.make_async_copy(
            pool.at[pt_ref[p, r]], held.at[r, pl.ds(p * page_len, page_len)], in_sem.at[r, p]
        )

    def send(r):
        to_z, to_x = targets[r] // side, targets[r] % side
        shift_x, shift_z = (to_x - my_x) & (side - 1), (to_z - my_z) & (side - 1)
        live = targets[r] >= 0
        for n in range(side):

            @pl.when(live & (shift_x == n))
            def _():
                pltpu.make_async_copy(
                    held.at[r, pl.ds(0, half)], across[n].at[to_z * 2 + ranks[r]], across_sem.at[r]
                ).start()

            @pl.when(live & (shift_z == n))
            def _():
                pltpu.make_async_copy(
                    held.at[r, pl.ds(half, half)], down[n].at[to_x * 2 + ranks[r]], down_sem.at[r]
                ).start()

    for r in range(rows):
        for p in range(pages):
            fetching(r, p).start()
    for r in range(rows):
        for p in range(pages):
            fetching(r, p).wait()
        length = len_ref[r]
        base = pl.multiple_of((length // 16) * 16, 16)
        block = held[r, pl.ds(base, 16), :].astype(f32)
        token = kv_ref[r : r + 1, :].astype(f32)
        here = iota(block.shape, 0) == length - base
        held[r, pl.ds(base, 16), :] = jnp.where(here, token, block).astype(bf16)

        send(r)
        pltpu.make_async_copy(held.at[r], whole.at[r], whole_sem.at[r]).start()

    for r in range(rows):
        pltpu.make_async_copy(held.at[r], whole.at[r], whole_sem.at[r]).wait()
    for r in range(rows):

        @pl.when(targets[r] >= 0)
        def _():
            pltpu.make_async_copy(
                held.at[r, pl.ds(0, half)], across[0].at[0], across_sem.at[r]
            ).wait()
            pltpu.make_async_copy(
                held.at[r, pl.ds(half, half)], down[0].at[0], down_sem.at[r]
            ).wait()


def self_body(rows, scale, len_ref, query_ref, whole_ref, att_ref, split_ref):
    _, history, both = whole_ref.shape
    head = both // 2
    heads = query_ref.shape[1] // head
    for h in range(heads):
        split_ref[pl.ds(h, rows, stride=heads), :] = query_ref[:, h * head : (h + 1) * head].astype(
            f32
        )
    for r in range(rows):
        queries = split_ref[r * heads : (r + 1) * heads, :].astype(bf16)
        scores = against(queries, whole_ref[r, :, 0:head]) * scale
        scores = jnp.where(iota((heads, history), 1) <= len_ref[r], scores, very_low)
        weights = jnp.exp(scores - jnp.max(scores, axis=1, keepdims=True))
        total = jnp.sum(weights, axis=1, keepdims=True)
        blended = jnp.dot(weights.astype(bf16), whole_ref[r, :, head:], preferred_element_type=f32)
        att_ref[r * heads : (r + 1) * heads, :] = (blended / total).astype(bf16)


def cross_body(
    rows, scale, mig_ref, asked_ref, image_row_ref, cache_ref, att_ref, stream_ref, out_ref,
    sorted_ref, part_ref, split_ref,
):
    images, _, both = cache_ref.shape
    head = both // 2
    everyone = asked_ref.shape[0]
    width = asked_ref.shape[1] - LANES
    heads = width // head
    group = everyone // images
    square = (everyone, everyone)
    image_row = image_row_ref[...]
    diagonal = iota(square, 1) == iota(square, 0)
    image_col = jnp.sum(
        jnp.where(diagonal, image_row.astype(f32), 0.0), axis=1, keepdims=True
    ).astype(i32)
    same = (image_col == image_row) & (iota(square, 1) < iota(square, 0))
    rank = jnp.sum(jnp.where(same, 1.0, 0.0), axis=1, keepdims=True).astype(i32)
    by_image = (iota(square, 1) == image_col * group + rank).astype(f32).astype(bf16)
    slot = asked_ref[:, width : width + 1].astype(f32).astype(i32)
    by_slot = (iota(square, 1) == slot).astype(f32).astype(bf16)
    sorted_ref[...] = onto(by_image, asked_ref[:, 0:width]).astype(bf16)
    order = onto(by_slot, by_image).astype(bf16)
    stacked = heads * group
    lane = iota((stacked, LANES), 1)
    head_of = iota((stacked, LANES), 0) // group
    for i in range(images):
        at = slice(i * group, (i + 1) * group)
        queries = jnp.concatenate(
            [sorted_ref[at, h * head : (h + 1) * head] for h in range(heads)], axis=0
        )
        scores = against(queries, cache_ref[i, :, 0:head]) * scale
        top = jnp.max(scores, axis=1, keepdims=True)
        top_hi = top.astype(bf16).astype(f32)
        top_lo = (top - top_hi).astype(bf16).astype(f32)
        weights = jnp.exp(scores - (top_hi + top_lo))
        total = jnp.sum(weights, axis=1, keepdims=True)
        total_hi = total.astype(bf16).astype(f32)
        total_lo = (total - total_hi).astype(bf16).astype(f32)
        blended = jnp.dot(weights.astype(bf16), cache_ref[i, :, head:], preferred_element_type=f32)
        blended = (blended / total).astype(bf16)
        about = jnp.zeros((stacked, LANES), f32)
        for n, stat in enumerate((top_hi, top_lo, total_hi, total_lo)):
            about = jnp.where(lane == n * heads + head_of, stat, about)
        packed = about[0:group]
        for h in range(1, heads):
            packed = packed + about[h * group : (h + 1) * group]
        for h in range(heads):
            part_ref[at, h * head : (h + 1) * head] = blended[h * group : (h + 1) * group]
        part_ref[at, width : width + LANES] = packed.astype(bf16)
    out_ref[:, 0 : width + LANES] = jnp.dot(
        order, part_ref[...], preferred_element_type=f32
    ).astype(bf16)
    targets, ranks = ranks_of(mig_ref, rows)
    chunks = stream_ref.shape[1] // LANES
    for c in range(chunks):
        split_ref[pl.ds(c, rows, stride=chunks), :] = stream_ref[
            :, c * LANES : (c + 1) * LANES
        ].astype(f32)
    lane_a = iota((1, rows * heads), 1)
    lane_s = iota((1, rows * chunks), 1)
    to_a = jnp.full(lane_a.shape, -1, i32)
    to_s = jnp.full(lane_s.shape, -1, i32)
    for r in range(rows):
        live = targets[r] >= 0
        base_a = jnp.where(live, targets[r] * rows + ranks[r] * heads, -rows * 64)
        base_s = jnp.where(live, targets[r] * rows + ranks[r] * chunks, -rows * 64)
        to_a = jnp.where(lane_a // heads == r, base_a + lane_a % heads, to_a)
        to_s = jnp.where(lane_s // chunks == r, base_s + lane_s % chunks, to_s)
    pick_a = (iota((everyone, rows * heads), 0) == to_a).astype(f32).astype(bf16)
    pick_s = (iota((everyone, rows * chunks), 0) == to_s).astype(f32).astype(bf16)
    at = width + LANES
    out_ref[:, at : at + LANES] = jnp.dot(
        pick_a, att_ref[...], preferred_element_type=f32
    ).astype(bf16)
    out_ref[:, at + LANES : at + 2 * LANES] = jnp.dot(
        pick_s, split_ref[...].astype(bf16), preferred_element_type=f32
    ).astype(bf16)


def settle_body(
    rows, me_ref, asked_ref, came_ref, att_ref, cross_ref, stream_ref, source_ref, coef_ref
):
    sources = came_ref.shape[0]
    everyone = asked_ref.shape[0]
    width = asked_ref.shape[1] - LANES
    heads = width // LANES
    chunks = stream_ref.shape[1] // LANES
    tall = (everyone, LANES)
    slot = asked_ref[:, width : width + 1].astype(f32).astype(i32)
    rank = asked_ref[:, width + 1 : width + 2].astype(f32).astype(i32)
    lane = iota(tall, 1)
    source = iota(tall, 0) // rows
    match = ((slot - me_ref[0] * rows == lane) & (lane < rows)).astype(f32).astype(bf16)
    facts = jnp.where(lane == 0, source * 2 + rank, 0)
    facts = jnp.where(lane == 1, source * rows + rank * heads, facts)
    facts = jnp.where(lane == 2, source * rows + rank * chunks, facts)
    facts = jnp.where(lane == 3, 1, facts).astype(f32).astype(bf16)
    by_lane = onto(facts, match)
    source_ref[...] = jnp.where(by_lane[3:4] > 0.5, by_lane[0:1], -1.0).astype(i32) + jnp.zeros(
        source_ref.shape, i32
    )
    by_row = onto(match, facts)[0:rows]
    live = by_row[:, 3:4] > 0.5
    base_a = jnp.where(live, by_row[:, 1:2], -4096.0).astype(i32)
    base_s = jnp.where(live, by_row[:, 2:3], -4096.0).astype(i32)
    column = iota((rows, everyone), 1)
    at = width + LANES
    own_a = came_ref[:, :, at : at + LANES].reshape(everyone, LANES)
    own_s = came_ref[:, :, at + LANES : at + 2 * LANES].reshape(everyone, LANES)
    for h in range(heads):
        pick = (column == base_a + h).astype(f32).astype(bf16)
        att_ref[:, h * LANES : (h + 1) * LANES] = jnp.dot(
            pick, own_a, preferred_element_type=f32
        ).astype(bf16)
    for c in range(chunks):
        pick = (column == base_s + c).astype(f32).astype(bf16)
        stream_ref[:, c * LANES : (c + 1) * LANES] = jnp.dot(
            pick, own_s, preferred_element_type=f32
        ).astype(bf16)
    highest = None
    for s in range(sources):
        about = came_ref[s, :, width : width + LANES].astype(f32)
        about = about + pltpu.roll(about, LANES - heads, 1)
        coef_ref[s] = about
        highest = about if s == 0 else jnp.maximum(highest, about)
    total = jnp.zeros((rows, LANES), f32)
    for s in range(sources):
        about = coef_ref[s]
        share = jnp.exp(about - highest) * pltpu.roll(about, LANES - 2 * heads, 1)
        coef_ref[s] = share
        total = total + share
    over = jnp.where(live, 1.0 / total, 0.0)
    for h in range(heads):
        blended = jnp.zeros((rows, LANES), f32)
        for s in range(sources):
            part = came_ref[s, :, h * LANES : (h + 1) * LANES].astype(f32)
            blended = blended + coef_ref[s][:, h : h + 1] * part
        blended = jnp.where(live, blended * over[:, h : h + 1], 0.0)
        cross_ref[:, h * LANES : (h + 1) * LANES] = blended.astype(bf16)


def project_body(me_ref, att_ref, cross_ref, self_w_ref, cross_w_ref, out_ref):
    rows = att_ref.shape[0]
    out_ref[0, 0:rows] = jnp.dot(att_ref[...], self_w_ref[...], preferred_element_type=f32)
    out_ref[0, rows : 2 * rows] = jnp.dot(
        cross_ref[...], cross_w_ref[...], preferred_element_type=f32
    )


def mix_body(side, me_ref, *refs):
    sent_x, sent_z = refs[:side], refs[side : 2 * side]
    next_z, next_x = refs[2 * side : 3 * side - 1], refs[3 * side - 1 : 4 * side - 2]
    held, in_sem, out_sem = refs[4 * side - 2 :]
    mine = me_ref[0] // side, me_ref[0] % side
    moves = []
    for here, came, onward in ((mine[0], sent_x, next_z), (mine[1], sent_z, next_x)):
        for shift in range(1, side):
            for n in range(side):
                at = ((here + shift) & (side - 1)) * 2
                moves.append((came[n].at[pl.ds(at, 2)], onward[shift - 1].at[pl.ds(2 * n, 2)]))
    for n, (source, _) in enumerate(moves):
        pltpu.make_async_copy(source, held.at[n], in_sem.at[n]).start()
    for n, (source, target) in enumerate(moves):
        pltpu.make_async_copy(source, held.at[n], in_sem.at[n]).wait()
        pltpu.make_async_copy(held.at[n], target, out_sem.at[n]).start()
    for n, (_, target) in enumerate(moves):
        pltpu.make_async_copy(held.at[n], target, out_sem.at[n]).wait()


def place_body(side, source_ref, me_ref, *refs):
    near_x, far_z = refs[:side], refs[side : 2 * side - 1]
    near_z, far_x = refs[2 * side - 1 : 3 * side - 1], refs[3 * side - 1 : 4 * side - 2]
    out, held, first_sem, last_sem, out_sem = refs[4 * side - 2 :]
    rows, history, _ = held.shape
    half = history // 2
    my_z, my_x = me_ref[0] // side, me_ref[0] % side

    def fetch(ref, at, t, begin, sem):
        return pltpu.make_async_copy(ref.at[at], held.at[t, pl.ds(begin, half)], sem.at[t])

    def begin(t, carry):
        code = source_ref[0, t]
        live = code >= 0
        code = jnp.maximum(code, 0)
        source, rank = code // 2, code % 2
        shift_z = (my_z - source // side) & (side - 1)
        shift_x = (my_x - source % side) & (side - 1)
        for n in range(side):

            @pl.when(live & (shift_z == 0) & (shift_x == n))
            def _():
                fetch(near_x[n], my_z * 2 + rank, t, 0, first_sem).start()

            @pl.when(live & (shift_x == 0) & (shift_z == n))
            def _():
                fetch(near_z[n], my_x * 2 + rank, t, half, last_sem).start()

        for n in range(1, side):

            @pl.when(live & (shift_z == n))
            def _():
                fetch(far_z[n - 1], shift_x * 2 + rank, t, 0, first_sem).start()

            @pl.when(live & (shift_x == n))
            def _():
                fetch(far_x[n - 1], shift_z * 2 + rank, t, half, last_sem).start()

        @pl.when(jnp.logical_not(live))
        def _():
            held[t] = jnp.zeros(held.shape[1:], bf16)

        return carry

    def finish(t, carry):
        @pl.when(source_ref[0, t] >= 0)
        def _():
            fetch(near_x[0], 0, t, 0, first_sem).wait()
            fetch(near_z[0], 0, t, half, last_sem).wait()

        pltpu.make_async_copy(held.at[t], out.at[t], out_sem.at[t]).start()
        return carry

    lax.fori_loop(0, rows, begin, 0)
    lax.fori_loop(0, rows, finish, 0)
    for t in range(rows):
        pltpu.make_async_copy(held.at[t], out.at[t], out_sem.at[t]).wait()


def in_order(found, shifts):
    return [found[0]] + [found[1 + shifts.index(n)] for n in range(1, len(found))]


def per_device(
    stream,
    self_query,
    new_kv,
    cache_pool,
    page_table,
    lengths,
    migration,
    image_of,
    cross_query,
    image_cache,
    self_output,
    cross_output,
    cross_gate,
):
    rows, width = cross_query.shape
    devices = lax.axis_size("rows")
    columns = lax.axis_size("heads")
    everyone = rows * devices
    pages = page_table.shape[1]
    pool_pages, page_len, _, both = cache_pool.shape
    head = both // 2
    heads = width // head
    history = pages * page_len
    images, tokens = image_cache.shape[:2]
    part = stream.shape[1]
    chunks = part // LANES
    scale = 1.0 / math.sqrt(head)
    out_width = self_output.shape[1]
    shape = jax.ShapeDtypeStruct
    mig = migration.T
    my_row = lax.axis_index("rows").astype(i32)[None]
    my_column = lax.axis_index("heads").astype(i32)[None]

    packed = pl.pallas_call(
        functools.partial(pack_body, rows),
        out_shape=shape((devices, rows, width + LANES), bf16),
        in_specs=[smem(), vmem()],
        out_specs=vmem(),
        name="pack",
    )(mig, cross_query)
    asked = lax.all_to_all(packed, "rows", 0, 0, tiled=True).reshape(everyone, width + LANES)

    side = math.isqrt(devices)
    shifts = (1, *range(side - 1, 1, -1))
    half = history // 2
    bucket = shape((2 * side, half, both), bf16)
    *buckets, whole = pl.pallas_call(
        functools.partial(own_body, rows, pages, page_len, side),
        out_shape=(*([bucket] * (2 * side)), shape((rows, history, both), bf16)),
        in_specs=[smem(), smem(), smem(), smem(), anywhere(), vmem()],
        out_specs=(*([anywhere()] * (2 * side)), anywhere()),
        scratch_shapes=[
            VMEM((rows, history, both), bf16),
            pltpu.SemaphoreType.DMA((rows, pages)),
            pltpu.SemaphoreType.DMA((rows,)),
            pltpu.SemaphoreType.DMA((rows,)),
            pltpu.SemaphoreType.DMA((rows,)),
        ],
        compiler_params=pltpu.CompilerParams(vmem_limit_bytes=61 << 20),
        cost_estimate=pl.CostEstimate(
            flops=0, bytes_accessed=6 * rows * history * both, transcendentals=0
        ),
        name="own",
    )(
        page_table.T,
        lengths,
        mig,
        my_row,
        cache_pool.reshape(pool_pages, page_len, both),
        new_kv.reshape(rows, both),
    )
    attended = pl.pallas_call(
        functools.partial(self_body, rows, scale),
        out_shape=shape((rows * heads, head), bf16),
        in_specs=[smem(), vmem(), vmem()],
        out_specs=vmem(),
        scratch_shapes=[VMEM((rows * heads, head), f32)],
        cost_estimate=pl.CostEstimate(
            flops=4 * rows * heads * history * head,
            bytes_accessed=2 * rows * history * both,
            transcendentals=rows * heads * history,
        ),
        name="attend",
    )(lengths, self_query, whole)

    def along(dz, dx):
        return [
            (z * side + x, ((z + dz) % side) * side + (x + dx) % side)
            for z in range(side)
            for x in range(side)
        ]

    near_x, near_z = [buckets[0]], [buckets[side]]
    for n in shifts:
        near_x.append(lax.ppermute(buckets[n], "rows", along(0, n)))
        near_z.append(lax.ppermute(buckets[side + n], "rows", along(n, 0)))
    near_x, near_z = in_order(near_x, shifts), in_order(near_z, shifts)

    message_width = width + 3 * LANES
    message = pl.pallas_call(
        functools.partial(cross_body, rows, scale),
        out_shape=shape((everyone, message_width), bf16),
        in_specs=[smem(), vmem(), vmem(), vmem(), vmem(), vmem()],
        out_specs=vmem(),
        scratch_shapes=[
            VMEM((everyone, width), bf16),
            VMEM((everyone, width + LANES), bf16),
            VMEM((rows * chunks, LANES), f32),
        ],
        cost_estimate=pl.CostEstimate(
            flops=4 * everyone * heads * tokens * head + 8 * everyone * everyone * width,
            bytes_accessed=2 * images * tokens * both + 4 * everyone * width,
            transcendentals=everyone * heads * tokens,
        ),
        compiler_params=pltpu.CompilerParams(vmem_limit_bytes=40 << 20),
        name="cross",
    )(
        mig,
        asked,
        image_of.reshape(1, everyone),
        image_cache.reshape(images, tokens, both),
        attended,
        stream,
    )
    came = lax.all_to_all(message.reshape(devices, rows, message_width), "rows", 0, 0, tiled=True)
    onward = pl.pallas_call(
        functools.partial(mix_body, side),
        out_shape=[bucket] * (2 * side - 2),
        in_specs=[smem()] + [anywhere()] * (2 * side),
        out_specs=[anywhere()] * (2 * side - 2),
        scratch_shapes=[
            VMEM((2 * side * (side - 1), 2, half, both), bf16),
            pltpu.SemaphoreType.DMA((2 * side * (side - 1),)),
            pltpu.SemaphoreType.DMA((2 * side * (side - 1),)),
        ],
        cost_estimate=pl.CostEstimate(
            flops=0, bytes_accessed=8 * rows * history * both, transcendentals=0
        ),
        name="mix",
    )(my_row, *near_x, *near_z)
    far_z, far_x = [None], [None]
    for n in shifts:
        far_z.append(lax.ppermute(onward[n - 1], "rows", along(n, 0)))
        far_x.append(lax.ppermute(onward[side - 1 + n - 1], "rows", along(0, n)))
    far_z, far_x = in_order(far_z, shifts)[1:], in_order(far_x, shifts)[1:]

    slot_attended, slot_cross, slot_stream, source = pl.pallas_call(
        functools.partial(settle_body, rows),
        out_shape=(
            shape((rows, width), bf16),
            shape((rows, width), bf16),
            shape((rows, part), bf16),
            shape((8, LANES), i32),
        ),
        in_specs=[smem(), vmem(), vmem()],
        out_specs=(vmem(), vmem(), vmem(), vmem()),
        scratch_shapes=[VMEM((devices, rows, LANES), f32)],
        cost_estimate=pl.CostEstimate(
            flops=4 * everyone * width,
            bytes_accessed=4 * everyone * width,
            transcendentals=everyone * LANES,
        ),
        compiler_params=pltpu.CompilerParams(vmem_limit_bytes=61 << 20),
        name="combine",
    )(my_row, asked, came)

    parts = pl.pallas_call(
        project_body,
        grid_spec=pltpu.PrefetchScalarGridSpec(
            num_scalar_prefetch=1,
            grid=(columns,),
            in_specs=[
                pl.BlockSpec((rows, width), lambda o, me: (0, 0)),
                pl.BlockSpec((rows, width), lambda o, me: (0, 0)),
                pl.BlockSpec((width, part), lambda o, me: (0, o)),
                pl.BlockSpec((width, part), lambda o, me: (0, o)),
            ],
            out_specs=pl.BlockSpec((1, 2 * rows, part), lambda o, me: (o, 0, 0)),
        ),
        out_shape=shape((columns, 2 * rows, part), f32),
        cost_estimate=pl.CostEstimate(
            flops=4 * rows * width * out_width,
            bytes_accessed=4 * width * out_width,
            transcendentals=0,
        ),
        compiler_params=pltpu.CompilerParams(vmem_limit_bytes=61 << 20),
        name="project",
    )(my_column, slot_attended, slot_cross, self_output, cross_output)
    parts = lax.all_to_all(parts, "heads", 0, 0, tiled=True)
    summed = jnp.sum(parts, axis=0)
    self_update = (slot_stream.astype(f32) + summed[:rows]).astype(bf16)
    cross_update = (jnp.tanh(cross_gate[0]) * summed[rows:]).astype(bf16)

    new_cache = pl.pallas_call(
        functools.partial(place_body, side),
        in_specs=[smem(), smem()] + [anywhere()] * (4 * side - 2),
        out_specs=anywhere(),
        out_shape=shape((rows, history, both), bf16),
        scratch_shapes=[
            VMEM((rows, history, both), bf16),
            pltpu.SemaphoreType.DMA((rows,)),
            pltpu.SemaphoreType.DMA((rows,)),
            pltpu.SemaphoreType.DMA((rows,)),
        ],
        cost_estimate=pl.CostEstimate(
            flops=0, bytes_accessed=4 * rows * history * both, transcendentals=0
        ),
        name="place",
    )(source, my_row, *near_x, *far_z, *near_z, *far_x)
    return (self_update, cross_update, new_cache.reshape(rows, history, 1, both))


def solution(mesh):
    in_specs = (
        P("rows", "heads"),
        P("rows", "heads"),
        P("rows", "heads", None),
        P("rows", None, "heads", None),
        P("rows", None),
        P("rows"),
        P("rows", None),
        P(),
        P("rows", "heads"),
        P(None, "rows", "heads", None),
        P("heads", None),
        P("heads", None),
        P(),
    )
    out_specs = (P("rows", "heads"), P("rows", "heads"), P("rows", None, "heads", None))

    return jax.shard_map(
        per_device, mesh=mesh, in_specs=in_specs, out_specs=out_specs, check_vma=False
    )
```

```python
import functools
import math

import jax
import jax.numpy as jnp
from jax import lax
from jax.experimental import pallas as pl
from jax.experimental.pallas import tpu as pltpu
from jax.sharding import PartitionSpec as P

very_low = -1e30
bf16 = jnp.bfloat16
f32 = jnp.float32
i32 = jnp.int32
LANES = 128
VMEM = pltpu.VMEM
SMEM = pltpu.SMEM


def vmem():
    return pl.BlockSpec(memory_space=VMEM)


def smem():
    return pl.BlockSpec(memory_space=SMEM)


def anywhere():
    return pl.BlockSpec(memory_space=pl.ANY)


def iota(shape, dim):
    return lax.broadcasted_iota(i32, shape, dim)


def onto(a, b):
    return lax.dot_general(a, b, (((0,), (0,)), ((), ())), preferred_element_type=f32)


def against(a, b):
    return lax.dot_general(a, b, (((1,), (1,)), ((), ())), preferred_element_type=f32)


def ranks_of(mig_ref, count):
    targets = [mig_ref[0, r] for r in range(count)]
    ranks = []
    for r in range(count):
        rank = jnp.int32(0)
        for e in range(r):
            rank = rank + (targets[e] == targets[r]).astype(i32)
        ranks.append(jnp.minimum(rank, 1))
    return targets, ranks


def pack_body(rows, mig_ref, query_ref, out_ref):
    targets, ranks = ranks_of(mig_ref, rows)
    width = query_ref.shape[1]
    sub, lane = iota((rows, LANES), 0), iota((rows, LANES), 1)
    about = jnp.full((rows, LANES), -1, i32)
    for r in range(rows):
        slot = jnp.where(targets[r] >= 0, targets[r] * rows + mig_ref[1, r], -1)
        about = jnp.where((sub == r) & (lane == 0), slot, about)
        about = jnp.where((sub == r) & (lane == 1), ranks[r], about)
    about = about.astype(f32).astype(bf16)
    for d in range(out_ref.shape[0]):
        out_ref[d, :, 0:width] = query_ref[...]
        out_ref[d, :, width : width + LANES] = about


def page_copies(rows, pages, page_len, pt_ref, pool, held, in_sem):
    return [
        [
            pltpu.make_async_copy(
                pool.at[pt_ref[p, r]], held.at[r, pl.ds(p * page_len, page_len)], in_sem.at[r, p]
            )
            for p in range(pages)
        ]
        for r in range(rows)
    ]


def write_token(r, len_ref, kv_ref, held):
    length = len_ref[r]
    base = pl.multiple_of((length // 16) * 16, 16)
    block = held[r, pl.ds(base, 16), :].astype(f32)
    token = kv_ref[r : r + 1, :].astype(f32)
    here = iota(block.shape, 0) == length - base
    held[r, pl.ds(base, 16), :] = jnp.where(here, token, block).astype(bf16)


def own_body(
    rows, pages, page_len, side, pt_ref, len_ref, mig_ref, me_ref, pool, kv_ref, *refs,
):
    across, down, (held, in_sem, across_sem, down_sem) = (
        refs[:side],
        refs[side : 2 * side],
        refs[2 * side :],
    )
    targets, ranks = ranks_of(mig_ref, rows)
    history = pages * page_len
    half = history // 2
    my_z, my_x = me_ref[0] // side, me_ref[0] % side

    copies = page_copies(rows, pages, page_len, pt_ref, pool, held, in_sem)

    def send(r):
        to_z, to_x = targets[r] // side, targets[r] % side
        shift_x, shift_z = (to_x - my_x) & (side - 1), (to_z - my_z) & (side - 1)
        live = targets[r] >= 0
        for n in range(side):

            @pl.when(live & (shift_x == n))
            def _():
                pltpu.make_async_copy(
                    held.at[r, pl.ds(0, half)], across[n].at[to_z * 2 + ranks[r]], across_sem.at[r]
                ).start()

            @pl.when(live & (shift_z == n))
            def _():
                pltpu.make_async_copy(
                    held.at[r, pl.ds(half, half)], down[n].at[to_x * 2 + ranks[r]], down_sem.at[r]
                ).start()

    for r in range(rows):
        for copy in copies[r]:
            copy.start()
    for r in range(rows):
        for copy in copies[r]:
            copy.wait()
        write_token(r, len_ref, kv_ref, held)
        send(r)

    for r in range(rows):

        @pl.when(targets[r] >= 0)
        def _():
            pltpu.make_async_copy(
                held.at[r, pl.ds(0, half)], across[0].at[0], across_sem.at[r]
            ).wait()
            pltpu.make_async_copy(
                held.at[r, pl.ds(half, half)], down[0].at[0], down_sem.at[r]
            ).wait()


def self_body(
    rows, pages, page_len, scale, pt_ref, len_ref, pool, kv_ref, query_ref, att_ref, held,
    split_ref, in_sem,
):
    _, history, both = held.shape
    head = both // 2
    heads = query_ref.shape[1] // head
    copies = page_copies(rows, pages, page_len, pt_ref, pool, held, in_sem)
    for r in range(rows):
        for copy in copies[r]:
            copy.start()
    for h in range(heads):
        split_ref[pl.ds(h, rows, stride=heads), :] = query_ref[:, h * head : (h + 1) * head].astype(
            f32
        )
    for r in range(rows):
        for copy in copies[r]:
            copy.wait()
        write_token(r, len_ref, kv_ref, held)
    for r in range(rows):
        queries = split_ref[r * heads : (r + 1) * heads, :].astype(bf16)
        scores = against(queries, held[r, :, 0:head]) * scale
        scores = jnp.where(iota((heads, history), 1) <= len_ref[r], scores, very_low)
        weights = jnp.exp(scores - jnp.max(scores, axis=1, keepdims=True))
        total = jnp.sum(weights, axis=1, keepdims=True)
        blended = jnp.dot(weights.astype(bf16), held[r, :, head:], preferred_element_type=f32)
        att_ref[r * heads : (r + 1) * heads, :] = (blended / total).astype(bf16)


def cross_body(
    rows, scale, mig_ref, asked_ref, image_row_ref, cache_ref, att_ref, stream_ref, out_ref,
    sorted_ref, part_ref, split_ref,
):
    images, _, both = cache_ref.shape
    head = both // 2
    everyone = asked_ref.shape[0]
    width = asked_ref.shape[1] - LANES
    heads = width // head
    group = everyone // images
    square = (everyone, everyone)
    image_row = image_row_ref[...]
    diagonal = iota(square, 1) == iota(square, 0)
    image_col = jnp.sum(
        jnp.where(diagonal, image_row.astype(f32), 0.0), axis=1, keepdims=True
    ).astype(i32)
    same = (image_col == image_row) & (iota(square, 1) < iota(square, 0))
    rank = jnp.sum(jnp.where(same, 1.0, 0.0), axis=1, keepdims=True).astype(i32)
    by_image = (iota(square, 1) == image_col * group + rank).astype(f32).astype(bf16)
    slot = asked_ref[:, width : width + 1].astype(f32).astype(i32)
    by_slot = (iota(square, 1) == slot).astype(f32).astype(bf16)
    sorted_ref[...] = onto(by_image, asked_ref[:, 0:width]).astype(bf16)
    order = onto(by_slot, by_image).astype(bf16)
    stacked = heads * group
    lane = iota((stacked, LANES), 1)
    head_of = iota((stacked, LANES), 0) // group
    for i in range(images):
        at = slice(i * group, (i + 1) * group)
        queries = jnp.concatenate(
            [sorted_ref[at, h * head : (h + 1) * head] for h in range(heads)], axis=0
        )
        scores = against(queries, cache_ref[i, :, 0:head]) * scale
        top = jnp.max(scores, axis=1, keepdims=True)
        top_hi = top.astype(bf16).astype(f32)
        top_lo = (top - top_hi).astype(bf16).astype(f32)
        weights = jnp.exp(scores - (top_hi + top_lo))
        total = jnp.sum(weights, axis=1, keepdims=True)
        total_hi = total.astype(bf16).astype(f32)
        total_lo = (total - total_hi).astype(bf16).astype(f32)
        blended = jnp.dot(weights.astype(bf16), cache_ref[i, :, head:], preferred_element_type=f32)
        blended = (blended / total).astype(bf16)
        about = jnp.zeros((stacked, LANES), f32)
        for n, stat in enumerate((top_hi, top_lo, total_hi, total_lo)):
            about = jnp.where(lane == n * heads + head_of, stat, about)
        packed = about[0:group]
        for h in range(1, heads):
            packed = packed + about[h * group : (h + 1) * group]
        for h in range(heads):
            part_ref[at, h * head : (h + 1) * head] = blended[h * group : (h + 1) * group]
        part_ref[at, width : width + LANES] = packed.astype(bf16)
    out_ref[:, 0 : width + LANES] = jnp.dot(
        order, part_ref[...], preferred_element_type=f32
    ).astype(bf16)
    targets, ranks = ranks_of(mig_ref, rows)
    chunks = stream_ref.shape[1] // LANES
    for c in range(chunks):
        split_ref[pl.ds(c, rows, stride=chunks), :] = stream_ref[
            :, c * LANES : (c + 1) * LANES
        ].astype(f32)
    lane_a = iota((1, rows * heads), 1)
    lane_s = iota((1, rows * chunks), 1)
    to_a = jnp.full(lane_a.shape, -1, i32)
    to_s = jnp.full(lane_s.shape, -1, i32)
    for r in range(rows):
        live = targets[r] >= 0
        base_a = jnp.where(live, targets[r] * rows + ranks[r] * heads, -rows * 64)
        base_s = jnp.where(live, targets[r] * rows + ranks[r] * chunks, -rows * 64)
        to_a = jnp.where(lane_a // heads == r, base_a + lane_a % heads, to_a)
        to_s = jnp.where(lane_s // chunks == r, base_s + lane_s % chunks, to_s)
    pick_a = (iota((everyone, rows * heads), 0) == to_a).astype(f32).astype(bf16)
    pick_s = (iota((everyone, rows * chunks), 0) == to_s).astype(f32).astype(bf16)
    at = width + LANES
    out_ref[:, at : at + LANES] = jnp.dot(
        pick_a, att_ref[...], preferred_element_type=f32
    ).astype(bf16)
    out_ref[:, at + LANES : at + 2 * LANES] = jnp.dot(
        pick_s, split_ref[...].astype(bf16), preferred_element_type=f32
    ).astype(bf16)


def settle_body(
    rows, me_ref, asked_ref, came_ref, att_ref, cross_ref, stream_ref, source_ref, coef_ref
):
    sources = came_ref.shape[0]
    everyone = asked_ref.shape[0]
    width = asked_ref.shape[1] - LANES
    heads = width // LANES
    chunks = stream_ref.shape[1] // LANES
    tall = (everyone, LANES)
    slot = asked_ref[:, width : width + 1].astype(f32).astype(i32)
    rank = asked_ref[:, width + 1 : width + 2].astype(f32).astype(i32)
    lane = iota(tall, 1)
    source = iota(tall, 0) // rows
    match = ((slot - me_ref[0] * rows == lane) & (lane < rows)).astype(f32).astype(bf16)
    facts = jnp.where(lane == 0, source * 2 + rank, 0)
    facts = jnp.where(lane == 1, source * rows + rank * heads, facts)
    facts = jnp.where(lane == 2, source * rows + rank * chunks, facts)
    facts = jnp.where(lane == 3, 1, facts).astype(f32).astype(bf16)
    by_lane = onto(facts, match)
    source_ref[...] = jnp.where(by_lane[3:4] > 0.5, by_lane[0:1], -1.0).astype(i32) + jnp.zeros(
        source_ref.shape, i32
    )
    by_row = onto(match, facts)[0:rows]
    live = by_row[:, 3:4] > 0.5
    base_a = jnp.where(live, by_row[:, 1:2], -4096.0).astype(i32)
    base_s = jnp.where(live, by_row[:, 2:3], -4096.0).astype(i32)
    column = iota((rows, everyone), 1)
    at = width + LANES
    own_a = came_ref[:, :, at : at + LANES].reshape(everyone, LANES)
    own_s = came_ref[:, :, at + LANES : at + 2 * LANES].reshape(everyone, LANES)
    for h in range(heads):
        pick = (column == base_a + h).astype(f32).astype(bf16)
        att_ref[:, h * LANES : (h + 1) * LANES] = jnp.dot(
            pick, own_a, preferred_element_type=f32
        ).astype(bf16)
    for c in range(chunks):
        pick = (column == base_s + c).astype(f32).astype(bf16)
        stream_ref[:, c * LANES : (c + 1) * LANES] = jnp.dot(
            pick, own_s, preferred_element_type=f32
        ).astype(bf16)
    highest = None
    for s in range(sources):
        about = came_ref[s, :, width : width + LANES].astype(f32)
        about = about + pltpu.roll(about, LANES - heads, 1)
        coef_ref[s] = about
        highest = about if s == 0 else jnp.maximum(highest, about)
    total = jnp.zeros((rows, LANES), f32)
    for s in range(sources):
        about = coef_ref[s]
        share = jnp.exp(about - highest) * pltpu.roll(about, LANES - 2 * heads, 1)
        coef_ref[s] = share
        total = total + share
    over = jnp.where(live, 1.0 / total, 0.0)
    for h in range(heads):
        blended = jnp.zeros((rows, LANES), f32)
        for s in range(sources):
            part = came_ref[s, :, h * LANES : (h + 1) * LANES].astype(f32)
            blended = blended + coef_ref[s][:, h : h + 1] * part
        blended = jnp.where(live, blended * over[:, h : h + 1], 0.0)
        cross_ref[:, h * LANES : (h + 1) * LANES] = blended.astype(bf16)


def project_body(me_ref, att_ref, cross_ref, self_w_ref, cross_w_ref, out_ref):
    rows = att_ref.shape[0]
    out_ref[0, 0:rows] = jnp.dot(att_ref[...], self_w_ref[...], preferred_element_type=f32)
    out_ref[0, rows : 2 * rows] = jnp.dot(
        cross_ref[...], cross_w_ref[...], preferred_element_type=f32
    )


def mix_body(side, me_ref, *refs):
    sent_x, sent_z = refs[:side], refs[side : 2 * side]
    next_z, next_x = refs[2 * side : 3 * side - 1], refs[3 * side - 1 : 4 * side - 2]
    held, in_sem, out_sem = refs[4 * side - 2 :]
    mine = me_ref[0] // side, me_ref[0] % side
    moves = []
    for here, came, onward in ((mine[0], sent_x, next_z), (mine[1], sent_z, next_x)):
        for shift in range(1, side):
            for n in range(side):
                at = ((here + shift) & (side - 1)) * 2
                moves.append((came[n].at[pl.ds(at, 2)], onward[shift - 1].at[pl.ds(2 * n, 2)]))
    for n, (source, _) in enumerate(moves):
        pltpu.make_async_copy(source, held.at[n], in_sem.at[n]).start()
    for n, (source, target) in enumerate(moves):
        pltpu.make_async_copy(source, held.at[n], in_sem.at[n]).wait()
        pltpu.make_async_copy(held.at[n], target, out_sem.at[n]).start()
    for n, (_, target) in enumerate(moves):
        pltpu.make_async_copy(held.at[n], target, out_sem.at[n]).wait()


def place_body(side, source_ref, me_ref, *refs):
    near_x, far_z = refs[:side], refs[side : 2 * side - 1]
    near_z, far_x = refs[2 * side - 1 : 3 * side - 1], refs[3 * side - 1 : 4 * side - 2]
    out, held, first_sem, last_sem, out_sem = refs[4 * side - 2 :]
    rows, history, _ = held.shape
    half = history // 2
    my_z, my_x = me_ref[0] // side, me_ref[0] % side

    def fetch(ref, at, t, begin, sem):
        return pltpu.make_async_copy(ref.at[at], held.at[t, pl.ds(begin, half)], sem.at[t])

    def begin(t, carry):
        code = source_ref[0, t]
        live = code >= 0
        code = jnp.maximum(code, 0)
        source, rank = code // 2, code % 2
        shift_z = (my_z - source // side) & (side - 1)
        shift_x = (my_x - source % side) & (side - 1)
        for n in range(side):

            @pl.when(live & (shift_z == 0) & (shift_x == n))
            def _():
                fetch(near_x[n], my_z * 2 + rank, t, 0, first_sem).start()

            @pl.when(live & (shift_x == 0) & (shift_z == n))
            def _():
                fetch(near_z[n], my_x * 2 + rank, t, half, last_sem).start()

        for n in range(1, side):

            @pl.when(live & (shift_z == n))
            def _():
                fetch(far_z[n - 1], shift_x * 2 + rank, t, 0, first_sem).start()

            @pl.when(live & (shift_x == n))
            def _():
                fetch(far_x[n - 1], shift_z * 2 + rank, t, half, last_sem).start()

        @pl.when(jnp.logical_not(live))
        def _():
            held[t] = jnp.zeros(held.shape[1:], bf16)

        return carry

    def finish(t, carry):
        @pl.when(source_ref[0, t] >= 0)
        def _():
            fetch(near_x[0], 0, t, 0, first_sem).wait()
            fetch(near_z[0], 0, t, half, last_sem).wait()

        pltpu.make_async_copy(held.at[t], out.at[t], out_sem.at[t]).start()
        return carry

    lax.fori_loop(0, rows, begin, 0)
    lax.fori_loop(0, rows, finish, 0)
    for t in range(rows):
        pltpu.make_async_copy(held.at[t], out.at[t], out_sem.at[t]).wait()


def in_order(found, shifts):
    return [found[0]] + [found[1 + shifts.index(n)] for n in range(1, len(found))]


def per_device(
    stream,
    self_query,
    new_kv,
    cache_pool,
    page_table,
    lengths,
    migration,
    image_of,
    cross_query,
    image_cache,
    self_output,
    cross_output,
    cross_gate,
):
    rows, width = cross_query.shape
    devices = lax.axis_size("rows")
    columns = lax.axis_size("heads")
    everyone = rows * devices
    pages = page_table.shape[1]
    pool_pages, page_len, _, both = cache_pool.shape
    head = both // 2
    heads = width // head
    history = pages * page_len
    images, tokens = image_cache.shape[:2]
    part = stream.shape[1]
    chunks = part // LANES
    scale = 1.0 / math.sqrt(head)
    out_width = self_output.shape[1]
    shape = jax.ShapeDtypeStruct
    mig = migration.T
    my_row = lax.axis_index("rows").astype(i32)[None]
    my_column = lax.axis_index("heads").astype(i32)[None]

    packed = pl.pallas_call(
        functools.partial(pack_body, rows),
        out_shape=shape((devices, rows, width + LANES), bf16),
        in_specs=[smem(), vmem()],
        out_specs=vmem(),
        name="pack",
    )(mig, cross_query)
    asked = lax.all_to_all(packed, "rows", 0, 0, tiled=True).reshape(everyone, width + LANES)

    side = math.isqrt(devices)
    shifts = (1, *range(side - 1, 1, -1))
    half = history // 2
    bucket = shape((2 * side, half, both), bf16)
    buckets = pl.pallas_call(
        functools.partial(own_body, rows, pages, page_len, side),
        out_shape=[bucket] * (2 * side),
        in_specs=[smem(), smem(), smem(), smem(), anywhere(), vmem()],
        out_specs=[anywhere()] * (2 * side),
        scratch_shapes=[
            VMEM((rows, history, both), bf16),
            pltpu.SemaphoreType.DMA((rows, pages)),
            pltpu.SemaphoreType.DMA((rows,)),
            pltpu.SemaphoreType.DMA((rows,)),
        ],
        compiler_params=pltpu.CompilerParams(vmem_limit_bytes=61 << 20),
        cost_estimate=pl.CostEstimate(
            flops=0, bytes_accessed=4 * rows * history * both, transcendentals=0
        ),
        name="own",
    )(
        page_table.T,
        lengths,
        mig,
        my_row,
        cache_pool.reshape(pool_pages, page_len, both),
        new_kv.reshape(rows, both),
    )
    attended = pl.pallas_call(
        functools.partial(self_body, rows, pages, page_len, scale),
        out_shape=shape((rows * heads, head), bf16),
        in_specs=[smem(), smem(), anywhere(), vmem(), vmem()],
        out_specs=vmem(),
        scratch_shapes=[
            VMEM((rows, history, both), bf16),
            VMEM((rows * heads, head), f32),
            pltpu.SemaphoreType.DMA((rows, pages)),
        ],
        compiler_params=pltpu.CompilerParams(vmem_limit_bytes=61 << 20),
        cost_estimate=pl.CostEstimate(
            flops=4 * rows * heads * history * head,
            bytes_accessed=2 * rows * history * both,
            transcendentals=rows * heads * history,
        ),
        name="attend",
    )(
        page_table.T,
        lengths,
        cache_pool.reshape(pool_pages, page_len, both),
        new_kv.reshape(rows, both),
        self_query,
    )

    def along(dz, dx):
        return [
            (z * side + x, ((z + dz) % side) * side + (x + dx) % side)
            for z in range(side)
            for x in range(side)
        ]

    near_x, near_z = [buckets[0]], [buckets[side]]
    for n in shifts:
        near_x.append(lax.ppermute(buckets[n], "rows", along(0, n)))
        near_z.append(lax.ppermute(buckets[side + n], "rows", along(n, 0)))
    near_x, near_z = in_order(near_x, shifts), in_order(near_z, shifts)

    message_width = width + 3 * LANES
    message = pl.pallas_call(
        functools.partial(cross_body, rows, scale),
        out_shape=shape((everyone, message_width), bf16),
        in_specs=[smem(), vmem(), vmem(), vmem(), vmem(), vmem()],
        out_specs=vmem(),
        scratch_shapes=[
            VMEM((everyone, width), bf16),
            VMEM((everyone, width + LANES), bf16),
            VMEM((rows * chunks, LANES), f32),
        ],
        cost_estimate=pl.CostEstimate(
            flops=4 * everyone * heads * tokens * head + 8 * everyone * everyone * width,
            bytes_accessed=2 * images * tokens * both + 4 * everyone * width,
            transcendentals=everyone * heads * tokens,
        ),
        compiler_params=pltpu.CompilerParams(vmem_limit_bytes=67_000_000),
        name="cross",
    )(
        mig,
        asked,
        image_of.reshape(1, everyone),
        image_cache.reshape(images, tokens, both),
        attended,
        stream,
    )
    came = lax.all_to_all(message.reshape(devices, rows, message_width), "rows", 0, 0, tiled=True)
    onward = pl.pallas_call(
        functools.partial(mix_body, side),
        out_shape=[bucket] * (2 * side - 2),
        in_specs=[smem()] + [anywhere()] * (2 * side),
        out_specs=[anywhere()] * (2 * side - 2),
        scratch_shapes=[
            VMEM((2 * side * (side - 1), 2, half, both), bf16),
            pltpu.SemaphoreType.DMA((2 * side * (side - 1),)),
            pltpu.SemaphoreType.DMA((2 * side * (side - 1),)),
        ],
        cost_estimate=pl.CostEstimate(
            flops=0, bytes_accessed=8 * rows * history * both, transcendentals=0
        ),
        name="mix",
    )(my_row, *near_x, *near_z)
    far_z, far_x = [None], [None]
    for n in shifts:
        far_z.append(lax.ppermute(onward[n - 1], "rows", along(n, 0)))
        far_x.append(lax.ppermute(onward[side - 1 + n - 1], "rows", along(0, n)))
    far_z, far_x = in_order(far_z, shifts)[1:], in_order(far_x, shifts)[1:]

    slot_attended, slot_cross, slot_stream, source = pl.pallas_call(
        functools.partial(settle_body, rows),
        out_shape=(
            shape((rows, width), bf16),
            shape((rows, width), bf16),
            shape((rows, part), bf16),
            shape((8, LANES), i32),
        ),
        in_specs=[smem(), vmem(), vmem()],
        out_specs=(vmem(), vmem(), vmem(), vmem()),
        scratch_shapes=[VMEM((devices, rows, LANES), f32)],
        cost_estimate=pl.CostEstimate(
            flops=4 * everyone * width,
            bytes_accessed=4 * everyone * width,
            transcendentals=everyone * LANES,
        ),
        compiler_params=pltpu.CompilerParams(vmem_limit_bytes=67_000_000),
        name="combine",
    )(my_row, asked, came)

    parts = pl.pallas_call(
        project_body,
        grid_spec=pltpu.PrefetchScalarGridSpec(
            num_scalar_prefetch=1,
            grid=(columns,),
            in_specs=[
                pl.BlockSpec((rows, width), lambda o, me: (0, 0)),
                pl.BlockSpec((rows, width), lambda o, me: (0, 0)),
                pl.BlockSpec((width, part), lambda o, me: (0, o)),
                pl.BlockSpec((width, part), lambda o, me: (0, o)),
            ],
            out_specs=pl.BlockSpec((1, 2 * rows, part), lambda o, me: (o, 0, 0)),
        ),
        out_shape=shape((columns, 2 * rows, part), f32),
        cost_estimate=pl.CostEstimate(
            flops=4 * rows * width * out_width,
            bytes_accessed=4 * width * out_width,
            transcendentals=0,
        ),
        compiler_params=pltpu.CompilerParams(vmem_limit_bytes=67_000_000),
        name="project",
    )(my_column, slot_attended, slot_cross, self_output, cross_output)
    parts = lax.all_to_all(parts, "heads", 0, 0, tiled=True)
    summed = jnp.sum(parts, axis=0)
    self_update = (slot_stream.astype(f32) + summed[:rows]).astype(bf16)
    cross_update = (jnp.tanh(cross_gate[0]) * summed[rows:]).astype(bf16)

    new_cache = pl.pallas_call(
        functools.partial(place_body, side),
        in_specs=[smem(), smem()] + [anywhere()] * (4 * side - 2),
        out_specs=anywhere(),
        out_shape=shape((rows, history, both), bf16),
        scratch_shapes=[
            VMEM((rows, history, both), bf16),
            pltpu.SemaphoreType.DMA((rows,)),
            pltpu.SemaphoreType.DMA((rows,)),
            pltpu.SemaphoreType.DMA((rows,)),
        ],
        cost_estimate=pl.CostEstimate(
            flops=0, bytes_accessed=4 * rows * history * both, transcendentals=0
        ),
        name="place",
    )(source, my_row, *near_x, *far_z, *near_z, *far_x)
    return (self_update, cross_update, new_cache.reshape(rows, history, 1, both))


def solution(mesh):
    in_specs = (
        P("rows", "heads"),
        P("rows", "heads"),
        P("rows", "heads", None),
        P("rows", None, "heads", None),
        P("rows", None),
        P("rows"),
        P("rows", None),
        P(),
        P("rows", "heads"),
        P(None, "rows", "heads", None),
        P("heads", None),
        P("heads", None),
        P(),
    )
    out_specs = (P("rows", "heads"), P("rows", "heads"), P("rows", None, "heads", None))

    return jax.shard_map(
        per_device, mesh=mesh, in_specs=in_specs, out_specs=out_specs, check_vma=False
    )
```
